512 devices in a mesh: chan: 32 (over z_hi, y, core), tm: 16 (over z_lo, x).
Axes of the slice: x: 4, y: 8, z: 8 (z_hi: 2, z_lo: 4; z = z_hi * 4 + z_lo), core: 2. Of those that a mesh axis runs over, the one named last changes fastest.
Arguments:
- recordings: bfloat16 [1024, 192, 4096], P('chan', 'tm'), may hold values from -6 to 6
- valid_mask: int32 [1024, 192], P('chan', 'tm'), may hold values 0 or 1
- src_chan: int32 [4], replicated, may hold values from 0 to 1023
Outputs:
- stacks: float32 [4, 1024, 4096], P(None, ('chan', 'tm'))
The draws below stay inside these ranges and needn't reach their ends.
All inputs are finite; a program needn't handle non-finite values. No bound on the sum of `valid_mask` on one device may be relied on, other than what follows from the above.
Results may differ from the reference program's by a relative error of at most 0.0048.
Values may be sent and summed in bfloat16 or wider, within the bound.
A program may use at most 128 MiB of HBM per device.

```python
import math
import jax
import jax.numpy as jnp
from jax import lax

NSRC = 4
SLOW = 32
FAST = 128
SAMPLES = 4096
NCH = 1024
NSEG = 192


def with_ends(drawn, key, smallest, largest):
    index_at = [jax.random.randint(jax.random.fold_in(key, axis), (), 0, length) for axis, length in enumerate(drawn.shape)]
    widest = drawn.shape.index(max(drawn.shape))
    next_to = index_at[:widest] + [(index_at[widest] + 1) % drawn.shape[widest]] + index_at[widest + 1:]
    return drawn.at[tuple(index_at)].set(smallest).at[tuple(next_to)].set(largest)


def block_levels(key, dims, pieces, least, top_value):
    def one(position, parts):
        heights = jax.random.uniform(jax.random.fold_in(jax.random.fold_in(key, 6), position), (parts,), jnp.float32, least / len(pieces), top_value / len(pieces))
        return jnp.repeat(jnp.exp(heights), dims[position] // parts).reshape((-1,) + (1,) * (len(dims) - position - 1))

    loudness = one(*pieces[0])
    for cut in pieces[1:]:
        loudness = loudness * one(*cut)
    return loudness


def scatter_about(own_key, extent, deviation, limit, pieces=(), kind=jnp.bfloat16):
    drawn = deviation * jax.random.normal(own_key, extent, jnp.float32)
    if pieces:
        drawn = drawn * block_levels(own_key, extent, pieces, -0.22, 0.18)
    return jnp.clip(drawn, -limit, limit).astype(kind)


def setup_inputs(seed: int = 0) -> dict:
    seeds = jax.random.split(jax.random.key(seed), 4)
    recordings = scatter_about(seeds[0], (NCH, NSEG, SAMPLES), 1.0, 6.0, ((0, 32), (1, 16)))
    valid_mask = with_ends((jax.random.randint(seeds[1], (NCH, NSEG), 0, 8) < 7).astype(jnp.int32), jax.random.fold_in(seeds[1], 1), 0, 1)
    src_chan = with_ends(jax.random.randint(seeds[2], (NSRC,), 0, NCH), jax.random.fold_in(seeds[2], 1), 0, NCH - 1).astype(jnp.int32)
    return dict(recordings=recordings, valid_mask=valid_mask, src_chan=src_chan)


def angles(rows_count, cols_count, period):
    left_index = jnp.arange(rows_count, dtype=jnp.int32)[:, None]
    right_index = jnp.arange(cols_count, dtype=jnp.int32)[None, :]
    return 2.0 * math.pi / period * (left_index * right_index % period).astype(jnp.float32)

def forward(tiles):
    slow_len = tiles.shape[1]
    fast_len = tiles.shape[2]
    samples = slow_len * fast_len
    slow_angle = angles(slow_len, slow_len, slow_len)
    cos_slow = jnp.cos(slow_angle).astype(jnp.bfloat16).astype(jnp.float32)
    sin_slow = jnp.sin(slow_angle).astype(jnp.bfloat16).astype(jnp.float32)
    tiles_wide = tiles.astype(jnp.float32)
    real_part = jnp.einsum('kn,rnm->rkm', cos_slow, tiles_wide, precision=lax.Precision.HIGHEST)
    imag_part = -jnp.einsum('kn,rnm->rkm', sin_slow, tiles_wide, precision=lax.Precision.HIGHEST)
    twist = angles(slow_len, fast_len, samples)
    twist_cos = jnp.cos(twist)
    twist_sin = jnp.sin(twist)
    z_real = (real_part * twist_cos + imag_part * twist_sin).astype(jnp.bfloat16).astype(jnp.float32)
    z_imag = (imag_part * twist_cos - real_part * twist_sin).astype(jnp.bfloat16).astype(jnp.float32)
    fast_angle = angles(fast_len, fast_len, fast_len)
    cos_fast = jnp.cos(fast_angle).astype(jnp.bfloat16).astype(jnp.float32)
    sin_fast = jnp.sin(fast_angle).astype(jnp.bfloat16).astype(jnp.float32)
    x_real = jnp.einsum('rkn,nm->rkm', z_real, cos_fast, precision=lax.Precision.HIGHEST) + jnp.einsum('rkn,nm->rkm', z_imag, sin_fast, precision=lax.Precision.HIGHEST)
    x_imag = jnp.einsum('rkn,nm->rkm', z_imag, cos_fast, precision=lax.Precision.HIGHEST) - jnp.einsum('rkn,nm->rkm', z_real, sin_fast, precision=lax.Precision.HIGHEST)
    power = x_real * x_real + x_imag * x_imag
    band_mean = lax.optimization_barrier(jnp.mean(power, axis=1))
    row_count = band_mean.shape[0]
    band_mean = lax.optimization_barrier(jnp.mean(band_mean.reshape(row_count, fast_len // 2, 2), axis=2))
    band_mean = jnp.repeat(band_mean, 2, axis=1)
    whiten_scale = lax.rsqrt(band_mean + 1e-06)[:, None, :]
    return ((x_real * whiten_scale).astype(jnp.bfloat16), (x_imag * whiten_scale).astype(jnp.bfloat16))

def inverse(z_real, z_imag, out_scale):
    slow_len = z_real.shape[-2]
    fast_len = z_real.shape[-1]
    samples = slow_len * fast_len
    back_angle = angles(fast_len, fast_len, fast_len)
    back_cos = jnp.cos(back_angle)
    back_sin = jnp.sin(back_angle)
    high = lax.Precision.HIGHEST
    v_real = jnp.einsum('...kn,nb->...kb', z_real, back_cos, precision=high) - jnp.einsum('...kn,nb->...kb', z_imag, back_sin, precision=high)
    v_imag = jnp.einsum('...kn,nb->...kb', z_real, back_sin, precision=high) + jnp.einsum('...kn,nb->...kb', z_imag, back_cos, precision=high)
    twist = angles(slow_len, fast_len, samples)
    twist_cos = jnp.cos(twist)
    twist_sin = jnp.sin(twist)
    w_real = v_real * twist_cos - v_imag * twist_sin
    w_imag = v_real * twist_sin + v_imag * twist_cos
    outer_angle = angles(slow_len, slow_len, slow_len)
    lagged = jnp.einsum('ak,...kb->...ab', jnp.cos(outer_angle), w_real, precision=high) - jnp.einsum('ak,...kb->...ab', jnp.sin(outer_angle), w_imag, precision=high)
    return lagged * out_scale

def reference(recordings, valid_mask, src_chan):

    def one_segment(carry, segment):
        tiles = lax.dynamic_index_in_dim(recordings, segment, 1, keepdims=False).reshape(NCH, SLOW, FAST)
        seg_weight = lax.dynamic_index_in_dim(valid_mask, segment, 1, keepdims=False).astype(jnp.float32)
        white_real, white_imag = forward(tiles)
        src_weight = seg_weight[src_chan][:, None, None]
        src_real = white_real[src_chan].astype(jnp.float32) * src_weight
        src_imag = white_imag[src_chan].astype(jnp.float32) * src_weight
        rec_real = white_real.astype(jnp.float32) * seg_weight[:, None, None]
        rec_imag = white_imag.astype(jnp.float32) * seg_weight[:, None, None]
        prod_real = src_real[:, None] * rec_real[None] + src_imag[:, None] * rec_imag[None]
        prod_imag = src_real[:, None] * rec_imag[None] - src_imag[:, None] * rec_real[None]
        return ((carry[0] + prod_real, carry[1] + prod_imag), None)
    start = jnp.zeros((NSRC, NCH, SLOW, FAST), jnp.float32)
    (cross_real, cross_imag), _ = lax.scan(one_segment, (start, start), jnp.arange(NSEG, dtype=jnp.int32))
    out_scale = 1.0 / math.sqrt(SLOW * FAST * NSEG)
    lagged = inverse(cross_real, cross_imag, out_scale)
    return lagged.reshape(NSRC, NCH, SLOW * FAST)
```

```python
import functools
import math

import jax
import jax.numpy as jnp
import numpy as np
from jax import lax
from jax.experimental import pallas as pl
from jax.experimental.pallas import tpu as pltpu
from jax.sharding import PartitionSpec as P

NSRC = 4
SLOW = 32
FAST = 128
BLOCK = 4
MESH = pl.DeviceIdType.MESH
VMEM_LIMIT = 60 * 1024 * 1024


def angles(rows_count, cols_count, period):
    left_index = np.arange(rows_count)[:, None]
    right_index = np.arange(cols_count)[None, :]
    return 2.0 * math.pi / period * (left_index * right_index % period)


def tables(out_scale):
    slow = angles(SLOW, SLOW, SLOW)
    fast = angles(FAST, FAST, FAST)
    twist = angles(SLOW, FAST, SLOW * FAST)
    first = np.kron(np.eye(8), np.concatenate([np.cos(slow), -np.sin(slow)], axis=0))
    second = np.block([[np.cos(fast), -np.sin(fast)], [np.sin(fast), np.cos(fast)]])
    back = np.block([[np.cos(fast), np.sin(fast)], [-np.sin(fast), np.cos(fast)]])
    outer = np.concatenate(
        [np.kron(np.eye(NSRC), np.cos(slow)), np.kron(np.eye(NSRC), -np.sin(slow))], axis=1
    )
    return (
        jnp.asarray(first, jnp.bfloat16),
        jnp.asarray(second, jnp.bfloat16),
        jnp.asarray(back, jnp.bfloat16),
        jnp.asarray(outer, jnp.bfloat16),
        jnp.asarray(np.stack([np.cos(twist), np.sin(twist)]), jnp.float32),
        jnp.asarray(np.stack([np.cos(twist), np.sin(twist)]) * out_scale, jnp.float32),
    )


def exchange(source, target, send, recv, device):
    return pltpu.make_async_remote_copy(
        src_ref=source,
        dst_ref=target,
        send_sem=send,
        recv_sem=recv,
        device_id=device,
        device_id_type=MESH,
    )


def greet(devices):
    barrier = pltpu.get_barrier_semaphore()
    for device in devices:
        pl.semaphore_signal(barrier, inc=1, device_id=device, device_id_type=MESH)
    pl.semaphore_wait(barrier, len(devices))


def share_kernel(
    ycount, own, out, pair_in, half, slices_in, part, across_in, whole, twin, s1, r1, s2, r2, s3, r3, s4, r4, s5, r5
):
    me = lax.axis_index("chan")
    core = me % 2
    y = me // 2 % ycount
    z = me // (2 * ycount)
    sibling = {"chan": me - core + (1 - core)}
    opposite = {"chan": ((1 - z) * ycount + y) * 2 + core}

    def along(step):
        return (y + step) % ycount

    def at(place):
        return {"chan": (z * ycount + place) * 2 + core}

    greet([sibling, opposite] + [at(along(step)) for step in range(1, ycount)])

    copy = exchange(own.at[1 - core], pair_in, s1, r1, sibling)
    copy.start()
    copy.wait()
    half[...] = own[core] + pair_in[...]

    copies = []
    for step in range(1, ycount):
        copies.append(
            exchange(
                half.at[along(step)],
                slices_in.at[step - 1],
                s2.at[step - 1],
                r2.at[step - 1],
                at(along(step)),
            )
        )
        copies[-1].start()
    for copy in copies:
        copy.wait()
    total = half[y]
    for step in range(ycount - 1):
        total = total + slices_in[step]
    part[...] = total

    copy = exchange(part, across_in, s3, r3, opposite)
    copy.start()
    copy.wait()
    whole[y] = part[...] + across_in[...]

    copies = []
    for step in range(1, ycount):
        copies.append(
            exchange(whole.at[y], whole.at[y], s4.at[step - 1], r4.at[step - 1], at(along(step)))
        )
        copies[-1].start()
    for copy in copies:
        copy.wait()

    copy = exchange(whole, twin, s5, r5, sibling)
    copy.start()
    out[core] = whole[...]
    copy.wait()
    out[1 - core] = twin[...]


def share(own, ycount):
    rows = own.shape[0]
    per = rows // (2 * ycount)
    shaped = own.reshape(2, ycount, per, FAST)
    half = (ycount, per, FAST)
    dma = pltpu.SemaphoreType.DMA
    spec = pl.BlockSpec(memory_space=pltpu.VMEM)
    out = pl.pallas_call(
        functools.partial(share_kernel, ycount),
        out_shape=jax.ShapeDtypeStruct(shaped.shape, own.dtype),
        in_specs=[spec],
        out_specs=spec,
        scratch_shapes=[
            pltpu.VMEM(half, own.dtype),
            pltpu.VMEM(half, own.dtype),
            pltpu.VMEM((ycount - 1, per, FAST), own.dtype),
            pltpu.VMEM((per, FAST), own.dtype),
            pltpu.VMEM((per, FAST), own.dtype),
            pltpu.VMEM(half, own.dtype),
            pltpu.VMEM(half, own.dtype),
            dma,
            dma,
            dma((ycount - 1,)),
            dma((ycount - 1,)),
            dma,
            dma,
            dma((ycount - 1,)),
            dma((ycount - 1,)),
            dma,
            dma,
        ],
        compiler_params=pltpu.CompilerParams(
            collective_id=0, has_side_effects=True, vmem_limit_bytes=VMEM_LIMIT
        ),
        name="share",
    )(shaped)
    return out.reshape(rows, FAST)


def gather_kernel(xcount, zcount, parts, out, x_in, mid, z_in, s1, r1, s2, r2):
    me = lax.axis_index("tm")
    x = me % xcount
    z = me // xcount

    def at(zpos, xpos):
        return {"tm": zpos * xcount + xpos}

    greet(
        [at(z, (x + step) % xcount) for step in range(1, xcount)]
        + [at((z + step) % zcount, x) for step in range(1, zcount)]
    )
    copies = []
    for step in range(1, xcount):
        to = (x + step) % xcount
        copies.append(
            exchange(parts.at[to], x_in.at[step - 1], s1.at[step - 1], r1.at[step - 1], at(z, to))
        )
        copies[-1].start()
    for copy in copies:
        copy.wait()

    def add_up(place):
        total = parts[x, place].astype(jnp.float32)
        for step in range(xcount - 1):
            total = total + x_in[step, place].astype(jnp.float32)
        return total

    copies = []
    for step in range(1, zcount):
        to = (z + step) % zcount
        mid[step - 1] = add_up(to).astype(jnp.bfloat16)
        copies.append(
            exchange(mid.at[step - 1], z_in.at[step - 1], s2.at[step - 1], r2.at[step - 1], at(to, x))
        )
        copies[-1].start()
    total = add_up(z)
    for copy in copies:
        copy.wait()
    for step in range(zcount - 1):
        total = total + z_in[step].astype(jnp.float32)
    out[...] = total


def gather(parts):
    xcount, zcount = parts.shape[:2]
    block = parts.shape[2:]
    dma = pltpu.SemaphoreType.DMA
    spec = pl.BlockSpec(memory_space=pltpu.VMEM)
    return pl.pallas_call(
        functools.partial(gather_kernel, xcount, zcount),
        out_shape=jax.ShapeDtypeStruct(block, jnp.float32),
        in_specs=[spec],
        out_specs=spec,
        scratch_shapes=[
            pltpu.VMEM((xcount - 1, zcount) + block, parts.dtype),
            pltpu.VMEM((zcount - 1,) + block, parts.dtype),
            pltpu.VMEM((zcount - 1,) + block, parts.dtype),
            dma((xcount - 1,)),
            dma((xcount - 1,)),
            dma((zcount - 1,)),
            dma((zcount - 1,)),
        ],
        compiler_params=pltpu.CompilerParams(
            collective_id=1, has_side_effects=True, vmem_limit_bytes=VMEM_LIMIT
        ),
        name="gather",
    )(parts)


def transform(tiles, weight, first, second, twist, keep):
    segs = tiles.shape[0] // SLOW
    lane = lax.broadcasted_iota(jnp.int32, (8, FAST), 1)
    for pair in range(segs // 16):
        base = pair * 512
        wide = jnp.concatenate(
            [tiles[pl.ds(base, 256), :], tiles[pl.ds(base + 256, 256), :]], axis=1
        )
        mixed = jnp.dot(first[...], wide, preferred_element_type=jnp.float32)
        for side in range(2):
            group = mixed[:, side * FAST : (side + 1) * FAST].reshape(8, 2 * SLOW, FAST)
            real_part = group[:, :SLOW]
            imag_part = group[:, SLOW:]
            twist_cos = twist[0][None]
            twist_sin = twist[1][None]
            z_real = (real_part * twist_cos + imag_part * twist_sin).astype(jnp.bfloat16)
            z_imag = (imag_part * twist_cos - real_part * twist_sin).astype(jnp.bfloat16)
            joined = jnp.concatenate([z_real, z_imag], axis=2).reshape(8 * SLOW, 2 * FAST)
            bins = jnp.dot(joined, second[...], preferred_element_type=jnp.float32)
            x_real = bins[:, :FAST].reshape(8, SLOW, FAST)
            x_imag = bins[:, FAST:].reshape(8, SLOW, FAST)
            power = jnp.sum(x_real * x_real + x_imag * x_imag, axis=1)
            other = jnp.where(
                lane % 2 == 0, pltpu.roll(power, FAST - 1, 1), pltpu.roll(power, 1, 1)
            )
            scale = lax.rsqrt((power + other) * (1.0 / (2 * SLOW)) + 1e-06)
            at = pair * 16 + side * 8
            if weight is not None:
                scale = scale * weight[pl.ds(at, 8), :]
            scale = scale[:, None, :]
            keep[0, pl.ds(at, 8)] = (x_real * scale).astype(jnp.bfloat16).astype(jnp.float32)
            keep[1, pl.ds(at, 8)] = (x_imag * scale).astype(jnp.bfloat16).astype(jnp.float32)


def stack_kernel(
    seg_count, tiles, weight, shared, first, second, back, outer, twist, turn, out, white, source
):
    @pl.when(pl.program_id(0) == 0)
    def _():
        transform(shared, None, first, second, twist, source)

    transform(tiles, weight, first, second, twist, white)

    def one_channel(chan, carry):
        strips = []
        for strip in range(SLOW // 8):
            rows = pl.ds(strip * 8, 8)
            real_sum = [None] * NSRC
            imag_sum = [None] * NSRC
            for seg in range(seg_count):
                w_real = white[0, chan * seg_count + seg, rows]
                w_imag = white[1, chan * seg_count + seg, rows]
                for src in range(NSRC):
                    s_real = source[0, src * seg_count + seg, rows]
                    s_imag = source[1, src * seg_count + seg, rows]
                    real_now = s_real * w_real + s_imag * w_imag
                    imag_now = s_real * w_imag - s_imag * w_real
                    first_seg = real_sum[src] is None
                    real_sum[src] = real_now if first_seg else real_sum[src] + real_now
                    imag_sum[src] = imag_now if first_seg else imag_sum[src] + imag_now
            strips.append((real_sum, imag_sum))
        cross_real = jnp.concatenate(
            [strips[k][0][src] for src in range(NSRC) for k in range(SLOW // 8)], axis=0
        )
        cross_imag = jnp.concatenate(
            [strips[k][1][src] for src in range(NSRC) for k in range(SLOW // 8)], axis=0
        )
        both = jnp.concatenate(
            [cross_real.astype(jnp.bfloat16), cross_imag.astype(jnp.bfloat16)], axis=1
        )
        v = jnp.dot(both, back[...], preferred_element_type=jnp.float32)
        v_real = v[:, :FAST].reshape(NSRC, SLOW, FAST)
        v_imag = v[:, FAST:].reshape(NSRC, SLOW, FAST)
        turn_cos = turn[0][None]
        turn_sin = turn[1][None]
        w_real = (v_real * turn_cos - v_imag * turn_sin).astype(jnp.bfloat16)
        w_imag = (v_real * turn_sin + v_imag * turn_cos).astype(jnp.bfloat16)
        tall = jnp.concatenate(
            [w_real.reshape(NSRC * SLOW, FAST), w_imag.reshape(NSRC * SLOW, FAST)], axis=0
        )
        lagged = jnp.dot(outer[...], tall, preferred_element_type=jnp.float32)
        out[chan // 2, 0, chan % 2] = lagged.astype(jnp.bfloat16).reshape(NSRC, SLOW, FAST)
        return carry

    lax.fori_loop(0, BLOCK, one_channel, 0)


def stack(tiles, weight, shared, chan_count, seg_count, xcount, zcount, out_scale):
    per = chan_count // (xcount * zcount)
    block_rows = BLOCK * seg_count * SLOW
    consts = tables(out_scale)
    turns = xcount // 2

    def whole(array):
        zeros = (0,) * array.ndim
        return pl.BlockSpec(array.shape, lambda i: zeros)

    return pl.pallas_call(
        functools.partial(stack_kernel, seg_count),
        grid=(chan_count // BLOCK,),
        out_shape=jax.ShapeDtypeStruct((xcount, zcount, per, NSRC, SLOW, FAST), jnp.bfloat16),
        in_specs=[
            pl.BlockSpec((block_rows, FAST), lambda i: (i, 0)),
            pl.BlockSpec((BLOCK * seg_count, FAST), lambda i: (i, 0)),
            whole(shared),
        ]
        + [whole(const) for const in consts],
        out_specs=pl.BlockSpec(
            (2, 1, per, NSRC, SLOW, FAST), lambda i: (i % turns, i // turns, 0, 0, 0, 0)
        ),
        scratch_shapes=[
            pltpu.VMEM((2, BLOCK * seg_count, SLOW, FAST), jnp.float32),
            pltpu.VMEM((2, NSRC * seg_count, SLOW, FAST), jnp.float32),
        ],
        compiler_params=pltpu.CompilerParams(
            dimension_semantics=("arbitrary",), vmem_limit_bytes=VMEM_LIMIT
        ),
        name="stack",
    )(tiles, weight, shared, *consts)


def per_device(recordings, valid_mask, src_chan):
    chan_count, seg_count, samples = recordings.shape
    group_count = lax.axis_size("tm")
    xcount = 4
    zcount = group_count // xcount
    ycount = lax.axis_size("chan") // 4
    tiled = recordings.reshape(chan_count, seg_count, SLOW, FAST)
    src_owner = src_chan // chan_count
    src_row = src_chan % chan_count
    out_scale = 1.0 / math.sqrt(samples * seg_count * group_count)
    mine = []
    for source in range(NSRC):
        own = lax.dynamic_index_in_dim(tiled, src_row[source], 0, keepdims=False)
        flags = lax.dynamic_index_in_dim(valid_mask, src_row[source], 0, keepdims=False)
        here = (flags != 0) & (lax.axis_index("chan") == src_owner[source])
        mine.append(jnp.where(here[:, None, None], own, jnp.zeros_like(own)))
    shared = share(jnp.stack(mine).reshape(NSRC * seg_count * SLOW, FAST), ycount)
    weight = jnp.broadcast_to(
        valid_mask.astype(jnp.float32).reshape(chan_count * seg_count, 1),
        (chan_count * seg_count, FAST),
    )
    parts = stack(
        tiled.reshape(chan_count * seg_count * SLOW, FAST),
        weight,
        shared,
        chan_count,
        seg_count,
        xcount,
        zcount,
        out_scale,
    )
    summed = gather(parts)
    return jnp.transpose(summed, (1, 0, 2, 3)).reshape(NSRC, chan_count // group_count, samples)


def solution(mesh):
    return jax.shard_map(
        per_device,
        mesh=mesh,
        in_specs=(P("chan", "tm", None), P("chan", "tm"), P()),
        out_specs=P(None, ("chan", "tm"), None),
        check_vma=False,
    )
```

```python
import functools
import math

import jax
import jax.numpy as jnp
import numpy as np
from jax import lax
from jax.experimental import pallas as pl
from jax.experimental.pallas import tpu as pltpu
from jax.sharding import PartitionSpec as P

NSRC = 4
SLOW = 32
FAST = 128
BLOCK = 4
MESH = pl.DeviceIdType.MESH
VMEM_LIMIT = 60 * 1024 * 1024


def angles(rows_count, cols_count, period):
    left_index = np.arange(rows_count)[:, None]
    right_index = np.arange(cols_count)[None, :]
    return 2.0 * math.pi / period * (left_index * right_index % period)


def tables(out_scale):
    slow = angles(SLOW, SLOW, SLOW)
    fast = angles(FAST, FAST, FAST)
    twist = angles(SLOW, FAST, SLOW * FAST)
    first = np.kron(np.eye(8), np.concatenate([np.cos(slow), -np.sin(slow)], axis=0))
    second = np.block([[np.cos(fast), -np.sin(fast)], [np.sin(fast), np.cos(fast)]])
    back = np.block([[np.cos(fast), np.sin(fast)], [-np.sin(fast), np.cos(fast)]])
    outer = np.concatenate(
        [np.kron(np.eye(NSRC), np.cos(slow)), np.kron(np.eye(NSRC), -np.sin(slow))], axis=1
    )
    return (
        jnp.asarray(first, jnp.bfloat16),
        jnp.asarray(second, jnp.bfloat16),
        jnp.asarray(back, jnp.bfloat16),
        jnp.asarray(outer, jnp.bfloat16),
        jnp.asarray(np.stack([np.cos(twist), np.sin(twist)]), jnp.float32),
        jnp.asarray(np.stack([np.cos(twist), np.sin(twist)]) * out_scale, jnp.float32),
    )


def exchange(source, target, send, recv, device):
    return pltpu.make_async_remote_copy(
        src_ref=source,
        dst_ref=target,
        send_sem=send,
        recv_sem=recv,
        device_id=device,
        device_id_type=MESH,
    )


def greet(devices):
    barrier = pltpu.get_barrier_semaphore()
    for device in devices:
        pl.semaphore_signal(barrier, inc=1, device_id=device, device_id_type=MESH)
    pl.semaphore_wait(barrier, len(devices))


def share_kernel(
    ycount, own, out, pair_in, half, slices_in, part, across_in, whole, twin, s1, r1, s2, r2, s3, r3, s4, r4, s5, r5
):
    me = lax.axis_index("chan")
    core = me % 2
    y = me // 2 % ycount
    z = me // (2 * ycount)
    sibling = {"chan": me - core + (1 - core)}
    opposite = {"chan": ((1 - z) * ycount + y) * 2 + core}

    def along(step):
        return (y + step) % ycount

    def at(place):
        return {"chan": (z * ycount + place) * 2 + core}

    greet([sibling, opposite] + [at(along(step)) for step in range(1, ycount)])

    copy = exchange(own.at[1 - core], pair_in, s1, r1, sibling)
    copy.start()
    copy.wait()
    half[...] = own[core] + pair_in[...]

    copies = []
    for step in range(1, ycount):
        copies.append(
            exchange(
                half.at[along(step)],
                slices_in.at[step - 1],
                s2.at[step - 1],
                r2.at[step - 1],
                at(along(step)),
            )
        )
        copies[-1].start()
    for copy in copies:
        copy.wait()
    total = half[y]
    for step in range(ycount - 1):
        total = total + slices_in[step]
    part[...] = total

    copy = exchange(part, across_in, s3, r3, opposite)
    copy.start()
    copy.wait()
    whole[y] = part[...] + across_in[...]

    copies = []
    for step in range(1, ycount):
        copies.append(
            exchange(whole.at[y], whole.at[y], s4.at[step - 1], r4.at[step - 1], at(along(step)))
        )
        copies[-1].start()
    for copy in copies:
        copy.wait()

    copy = exchange(whole, twin, s5, r5, sibling)
    copy.start()
    out[core] = whole[...]
    copy.wait()
    out[1 - core] = twin[...]


def share(own, ycount):
    rows = own.shape[0]
    per = rows // (2 * ycount)
    shaped = own.reshape(2, ycount, per, FAST)
    half = (ycount, per, FAST)
    dma = pltpu.SemaphoreType.DMA
    spec = pl.BlockSpec(memory_space=pltpu.VMEM)
    out = pl.pallas_call(
        functools.partial(share_kernel, ycount),
        out_shape=jax.ShapeDtypeStruct(shaped.shape, own.dtype),
        in_specs=[spec],
        out_specs=spec,
        scratch_shapes=[
            pltpu.VMEM(half, own.dtype),
            pltpu.VMEM(half, own.dtype),
            pltpu.VMEM((ycount - 1, per, FAST), own.dtype),
            pltpu.VMEM((per, FAST), own.dtype),
            pltpu.VMEM((per, FAST), own.dtype),
            pltpu.VMEM(half, own.dtype),
            pltpu.VMEM(half, own.dtype),
            dma,
            dma,
            dma((ycount - 1,)),
            dma((ycount - 1,)),
            dma,
            dma,
            dma((ycount - 1,)),
            dma((ycount - 1,)),
            dma,
            dma,
        ],
        compiler_params=pltpu.CompilerParams(
            collective_id=0, has_side_effects=True, vmem_limit_bytes=VMEM_LIMIT
        ),
        name="share",
    )(shaped)
    return out.reshape(rows, FAST)


def gather_kernel(xcount, zcount, parts, out, x_in, mid, z_in, s1, r1, s2, r2):
    me = lax.axis_index("tm")
    x = me % xcount
    z = me // xcount

    def at(zpos, xpos):
        return {"tm": zpos * xcount + xpos}

    greet(
        [at(z, (x + step) % xcount) for step in range(1, xcount)]
        + [at((z + step) % zcount, x) for step in range(1, zcount)]
    )
    copies = []
    for step in range(1, xcount):
        to = (x + step) % xcount
        copies.append(
            exchange(parts.at[to], x_in.at[step - 1], s1.at[step - 1], r1.at[step - 1], at(z, to))
        )
        copies[-1].start()
    for copy in copies:
        copy.wait()

    def add_up(place):
        total = parts[x, place].astype(jnp.float32)
        for step in range(xcount - 1):
            total = total + x_in[step, place].astype(jnp.float32)
        return total

    copies = []
    for step in range(1, zcount):
        to = (z + step) % zcount
        mid[step - 1] = add_up(to).astype(jnp.bfloat16)
        copies.append(
            exchange(mid.at[step - 1], z_in.at[step - 1], s2.at[step - 1], r2.at[step - 1], at(to, x))
        )
        copies[-1].start()
    total = add_up(z)
    for copy in copies:
        copy.wait()
    for step in range(zcount - 1):
        total = total + z_in[step].astype(jnp.float32)
    out[...] = total


def gather(parts):
    xcount, zcount = parts.shape[:2]
    block = parts.shape[2:]
    dma = pltpu.SemaphoreType.DMA
    spec = pl.BlockSpec(memory_space=pltpu.VMEM)
    return pl.pallas_call(
        functools.partial(gather_kernel, xcount, zcount),
        out_shape=jax.ShapeDtypeStruct(block, jnp.float32),
        in_specs=[spec],
        out_specs=spec,
        scratch_shapes=[
            pltpu.VMEM((xcount - 1, zcount) + block, parts.dtype),
            pltpu.VMEM((zcount - 1,) + block, parts.dtype),
            pltpu.VMEM((zcount - 1,) + block, parts.dtype),
            dma((xcount - 1,)),
            dma((xcount - 1,)),
            dma((zcount - 1,)),
            dma((zcount - 1,)),
        ],
        compiler_params=pltpu.CompilerParams(
            collective_id=1, has_side_effects=True, vmem_limit_bytes=VMEM_LIMIT
        ),
        name="gather",
    )(parts)


def transform(tiles, weight, first, second, twist, keep):
    segs = tiles.shape[0] // SLOW
    lane = lax.broadcasted_iota(jnp.int32, (8, FAST), 1)
    for pair in range(segs // 16):
        base = pair * 512
        wide = jnp.concatenate(
            [tiles[base : base + 256], tiles[base + 256 : base + 512]], axis=1
        )
        mixed = jnp.dot(first[...], wide, preferred_element_type=jnp.float32)
        for side in range(2):
            group = mixed[:, side * FAST : (side + 1) * FAST].reshape(8, 2 * SLOW, FAST)
            real_part = group[:, :SLOW]
            imag_part = group[:, SLOW:]
            twist_cos = twist[0][None]
            twist_sin = twist[1][None]
            z_real = (real_part * twist_cos + imag_part * twist_sin).astype(jnp.bfloat16)
            z_imag = (imag_part * twist_cos - real_part * twist_sin).astype(jnp.bfloat16)
            joined = jnp.concatenate([z_real, z_imag], axis=2).reshape(8 * SLOW, 2 * FAST)
            bins = jnp.dot(joined, second[...], preferred_element_type=jnp.float32)
            x_real = bins[:, :FAST].reshape(8, SLOW, FAST)
            x_imag = bins[:, FAST:].reshape(8, SLOW, FAST)
            power = jnp.sum(x_real * x_real + x_imag * x_imag, axis=1)
            other = jnp.where(
                lane % 2 == 0, pltpu.roll(power, FAST - 1, 1), pltpu.roll(power, 1, 1)
            )
            scale = lax.rsqrt((power + other) * (1.0 / (2 * SLOW)) + 1e-06)
            at = pair * 16 + side * 8
            if weight is not None:
                scale = scale * weight[pl.ds(at, 8), :]
            scale = scale[:, None, :]
            keep[0, pl.ds(at, 8)] = (x_real * scale).astype(jnp.bfloat16).astype(jnp.float32)
            keep[1, pl.ds(at, 8)] = (x_imag * scale).astype(jnp.bfloat16).astype(jnp.float32)


def stack_kernel(
    seg_count, tiles, weight, shared, first, second, back, outer, twist, turn, out, white, source
):
    @pl.when(pl.program_id(0) == 0)
    def _():
        transform(shared[...], None, first, second, twist, source)

    flat = tiles[...].reshape(BLOCK * seg_count * SLOW, FAST)
    transform(flat, weight, first, second, twist, white)

    def one_channel(chan, carry):
        strips = []
        for strip in range(SLOW // 8):
            rows = pl.ds(strip * 8, 8)
            real_sum = [None] * NSRC
            imag_sum = [None] * NSRC
            for seg in range(seg_count):
                w_real = white[0, seg * BLOCK + chan, rows]
                w_imag = white[1, seg * BLOCK + chan, rows]
                for src in range(NSRC):
                    s_real = source[0, src * seg_count + seg, rows]
                    s_imag = source[1, src * seg_count + seg, rows]
                    real_now = s_real * w_real + s_imag * w_imag
                    imag_now = s_real * w_imag - s_imag * w_real
                    first_seg = real_sum[src] is None
                    real_sum[src] = real_now if first_seg else real_sum[src] + real_now
                    imag_sum[src] = imag_now if first_seg else imag_sum[src] + imag_now
            strips.append((real_sum, imag_sum))
        cross_real = jnp.concatenate(
            [strips[k][0][src] for src in range(NSRC) for k in range(SLOW // 8)], axis=0
        )
        cross_imag = jnp.concatenate(
            [strips[k][1][src] for src in range(NSRC) for k in range(SLOW // 8)], axis=0
        )
        both = jnp.concatenate(
            [cross_real.astype(jnp.bfloat16), cross_imag.astype(jnp.bfloat16)], axis=1
        )
        v = jnp.dot(both, back[...], preferred_element_type=jnp.float32)
        v_real = v[:, :FAST].reshape(NSRC, SLOW, FAST)
        v_imag = v[:, FAST:].reshape(NSRC, SLOW, FAST)
        turn_cos = turn[0][None]
        turn_sin = turn[1][None]
        w_real = (v_real * turn_cos - v_imag * turn_sin).astype(jnp.bfloat16)
        w_imag = (v_real * turn_sin + v_imag * turn_cos).astype(jnp.bfloat16)
        tall = jnp.concatenate(
            [w_real.reshape(NSRC * SLOW, FAST), w_imag.reshape(NSRC * SLOW, FAST)], axis=0
        )
        lagged = jnp.dot(outer[...], tall, preferred_element_type=jnp.float32)
        out[chan // 2, 0, chan % 2] = lagged.astype(jnp.bfloat16).reshape(NSRC, SLOW, FAST)
        return carry

    lax.fori_loop(0, BLOCK, one_channel, 0)


def pick_kernel(src, flags, tiles, out):
    seg_count, chan_count = tiles.shape[0], flags.shape[0] // tiles.shape[0]
    want = src[pl.program_id(0)]
    here = want // chan_count == lax.axis_index("chan")
    row = want % chan_count
    for seg in range(seg_count):
        keep = here & (flags[seg * chan_count + row] != 0)
        factor = jnp.where(keep, 1.0, 0.0)
        out[0, seg] = (tiles[seg, 0].astype(jnp.float32) * factor).astype(out.dtype)


def pick(tiled, flags, src_chan):
    seg_count, chan_count = tiled.shape[:2]
    return pl.pallas_call(
        pick_kernel,
        grid_spec=pltpu.PrefetchScalarGridSpec(
            num_scalar_prefetch=2,
            grid=(NSRC,),
            in_specs=[
                pl.BlockSpec(
                    (seg_count, 1, SLOW, FAST),
                    lambda i, src, flags: (0, src[i] % chan_count, 0, 0),
                )
            ],
            out_specs=pl.BlockSpec(
                (1, seg_count, SLOW, FAST), lambda i, src, flags: (i, 0, 0, 0)
            ),
        ),
        out_shape=jax.ShapeDtypeStruct((NSRC, seg_count, SLOW, FAST), tiled.dtype),
        name="pick",
    )(src_chan, flags, tiled)


def stack(tiles, weight, shared, xcount, zcount, out_scale):
    seg_count, chan_count = tiles.shape[:2]
    per = chan_count // (xcount * zcount)
    consts = tables(out_scale)
    turns = xcount // 2

    def whole(array):
        zeros = (0,) * array.ndim
        return pl.BlockSpec(array.shape, lambda i: zeros)

    return pl.pallas_call(
        functools.partial(stack_kernel, seg_count),
        grid=(chan_count // BLOCK,),
        out_shape=jax.ShapeDtypeStruct((xcount, zcount, per, NSRC, SLOW, FAST), jnp.bfloat16),
        in_specs=[
            pl.BlockSpec((seg_count, BLOCK, SLOW, FAST), lambda i: (0, i, 0, 0)),
            pl.BlockSpec((BLOCK * seg_count, FAST), lambda i: (i, 0)),
            whole(shared),
        ]
        + [whole(const) for const in consts],
        out_specs=pl.BlockSpec(
            (2, 1, per, NSRC, SLOW, FAST), lambda i: (i % turns, i // turns, 0, 0, 0, 0)
        ),
        scratch_shapes=[
            pltpu.VMEM((2, BLOCK * seg_count, SLOW, FAST), jnp.float32),
            pltpu.VMEM((2, NSRC * seg_count, SLOW, FAST), jnp.float32),
        ],
        compiler_params=pltpu.CompilerParams(
            dimension_semantics=("arbitrary",), vmem_limit_bytes=VMEM_LIMIT
        ),
        name="stack",
    )(tiles, weight, shared, *consts)


def per_device(recordings, valid_mask, src_chan):
    chan_count, seg_count, samples = recordings.shape
    group_count = lax.axis_size("tm")
    xcount = 4
    zcount = group_count // xcount
    ycount = lax.axis_size("chan") // 4
    out_scale = 1.0 / math.sqrt(samples * seg_count * group_count)
    tiled = jnp.transpose(recordings, (1, 0, 2)).reshape(seg_count, chan_count, SLOW, FAST)
    flags = jnp.transpose(valid_mask)
    mine = pick(tiled, flags.reshape(-1), src_chan)
    shared = share(mine.reshape(NSRC * seg_count * SLOW, FAST), ycount)
    weight = flags.astype(jnp.float32).reshape(seg_count, chan_count // BLOCK, BLOCK)
    weight = jnp.transpose(weight, (1, 0, 2)).reshape(chan_count * seg_count, 1)
    weight = jnp.broadcast_to(weight, (chan_count * seg_count, FAST))
    parts = stack(tiled, weight, shared, xcount, zcount, out_scale)
    summed = gather(parts)
    return jnp.transpose(summed, (1, 0, 2, 3)).reshape(NSRC, chan_count // group_count, samples)


def solution(mesh):
    return jax.shard_map(
        per_device,
        mesh=mesh,
        in_specs=(P("chan", "tm", None), P("chan", "tm"), P()),
        out_specs=P(None, ("chan", "tm"), None),
        check_vma=False,
    )
```

```python
import functools
import math

import jax
import jax.numpy as jnp
import numpy as np
from jax import lax
from jax.experimental import pallas as pl
from jax.experimental.pallas import tpu as pltpu
from jax.sharding import PartitionSpec as P

NSRC = 4
SLOW = 32
FAST = 128
BLOCK = 4
MESH = pl.DeviceIdType.MESH
VMEM_LIMIT = 60 * 1024 * 1024


def angles(rows_count, cols_count, period):
    left_index = np.arange(rows_count)[:, None]
    right_index = np.arange(cols_count)[None, :]
    return 2.0 * math.pi / period * (left_index * right_index % period)


def tables(out_scale):
    slow = angles(SLOW, SLOW, SLOW)
    fast = angles(FAST, FAST, FAST)
    twist = angles(SLOW, FAST, SLOW * FAST)
    first = np.kron(np.eye(8), np.concatenate([np.cos(slow), -np.sin(slow)], axis=0))
    second = np.block([[np.cos(fast), -np.sin(fast)], [np.sin(fast), np.cos(fast)]])
    back = np.block([[np.cos(fast), np.sin(fast)], [-np.sin(fast), np.cos(fast)]])
    outer = np.concatenate(
        [np.kron(np.eye(NSRC), np.cos(slow)), np.kron(np.eye(NSRC), -np.sin(slow))], axis=1
    )
    return (
        jnp.asarray(first, jnp.bfloat16),
        jnp.asarray(second, jnp.bfloat16),
        jnp.asarray(back, jnp.bfloat16),
        jnp.asarray(outer, jnp.bfloat16),
        jnp.asarray(np.stack([np.cos(twist), np.sin(twist)]), jnp.float32),
        jnp.asarray(np.stack([np.cos(twist), np.sin(twist)]) * out_scale, jnp.float32),
    )


def exchange(source, target, send, recv, device):
    return pltpu.make_async_remote_copy(
        src_ref=source,
        dst_ref=target,
        send_sem=send,
        recv_sem=recv,
        device_id=device,
        device_id_type=MESH,
    )


def greet(devices):
    barrier = pltpu.get_barrier_semaphore()
    for device in devices:
        pl.semaphore_signal(barrier, inc=1, device_id=device, device_id_type=MESH)
    pl.semaphore_wait(barrier, len(devices))


def transform(tiles, weight, first, second, twist, store):
    lane = lax.broadcasted_iota(jnp.int32, (8, FAST), 1)
    for pair in range(tiles.shape[0] // 512):
        base = pair * 512
        wide = jnp.concatenate(
            [tiles[base : base + 256], tiles[base + 256 : base + 512]], axis=1
        )
        mixed = jnp.dot(first[...], wide, preferred_element_type=jnp.float32)
        for side in range(2):
            group = mixed[:, side * FAST : (side + 1) * FAST].reshape(8, 2 * SLOW, FAST)
            real_part = group[:, :SLOW]
            imag_part = group[:, SLOW:]
            twist_cos = twist[0][None]
            twist_sin = twist[1][None]
            z_real = (real_part * twist_cos + imag_part * twist_sin).astype(jnp.bfloat16)
            z_imag = (imag_part * twist_cos - real_part * twist_sin).astype(jnp.bfloat16)
            joined = jnp.concatenate([z_real, z_imag], axis=2).reshape(8 * SLOW, 2 * FAST)
            bins = jnp.dot(joined, second[...], preferred_element_type=jnp.float32)
            x_real = bins[:, :FAST].reshape(8, SLOW, FAST)
            x_imag = bins[:, FAST:].reshape(8, SLOW, FAST)
            power = jnp.sum(x_real * x_real + x_imag * x_imag, axis=1)
            other = jnp.where(
                lane % 2 == 0, pltpu.roll(power, FAST - 1, 1), pltpu.roll(power, 1, 1)
            )
            scale = lax.rsqrt((power + other) * (1.0 / (2 * SLOW)) + 1e-06)
            at = pair * 16 + side * 8
            if weight is not None:
                scale = scale * weight(at)
            scale = scale[:, None, :]
            store(
                at,
                (x_real * scale).astype(jnp.bfloat16).astype(jnp.float32),
                (x_imag * scale).astype(jnp.bfloat16).astype(jnp.float32),
            )


def whole_kernel(
    ycount, xcount, zcount,
    own, tiles, flags, eye, first, second, back, outer, twist, turn,
    out,
    white, source, weights,
    pair_in, half, slices_in, part, across_in, whole, twin,
    parts, x_in, mid, z_in,
    s1, r1, s2, r2, s3, r3, s4, r4, s5, r5, s6, r6, s7, r7,
):
    seg_count, chan_count = tiles.shape[:2]
    segs = seg_count * BLOCK
    me = lax.axis_index("chan")
    core = me % 2
    y = me // 2 % ycount
    z = me // (2 * ycount)
    sibling = {"chan": me - core + (1 - core)}
    opposite = {"chan": ((1 - z) * ycount + y) * 2 + core}
    spot = lax.axis_index("tm")
    sx = spot % xcount
    sz = spot // xcount

    def along(step):
        return (y + step) % ycount

    def at_y(place):
        return {"chan": (z * ycount + place) * 2 + core}

    def at_xz(zpos, xpos):
        return {"tm": zpos * xcount + xpos}

    greet(
        [sibling, opposite]
        + [at_y(along(step)) for step in range(1, ycount)]
        + [at_xz(sz, (sx + step) % xcount) for step in range(1, xcount)]
        + [at_xz((sz + step) % zcount, sx) for step in range(1, zcount)]
    )

    def forward(low, high):
        def one_block(block, carry):
            flat = tiles[:, pl.ds(block * BLOCK, BLOCK)].reshape(segs * SLOW, FAST)

            def weight(at):
                return weights[block, at : at + 8]

            def store(at, real, imag):
                white[0, block, at : at + 8] = real
                white[1, block, at : at + 8] = imag

            transform(flat, weight, first, second, twist, store)
            return carry

        lax.fori_loop(low, high, one_block, 0)

    copy = exchange(own.at[1 - core], pair_in, s1, r1, sibling)
    copy.start()
    spread = (flags[...].astype(jnp.float32)[:, None, :] * eye[...][None]).astype(jnp.bfloat16)
    rows = jnp.dot(
        spread.reshape(seg_count * chan_count, chan_count),
        jnp.ones((chan_count, FAST), jnp.bfloat16),
        preferred_element_type=jnp.float32,
    ).reshape(seg_count, chan_count, FAST)
    for block in range(chan_count // BLOCK):
        weights[block] = rows[:, block * BLOCK : (block + 1) * BLOCK].reshape(segs, FAST)
    forward(0, 1)
    copy.wait()
    half[...] = own[core] + pair_in[...]

    copies = []
    for step in range(1, ycount):
        to = along(step)
        copies.append(
            exchange(half.at[to], slices_in.at[step - 1], s2.at[step - 1], r2.at[step - 1], at_y(to))
        )
        copies[-1].start()
    forward(1, 3)
    for copy in copies:
        copy.wait()
    total = half[y]
    for step in range(ycount - 1):
        total = total + slices_in[step]
    part[...] = total

    copy = exchange(part, across_in, s3, r3, opposite)
    copy.start()
    forward(3, 5)
    copy.wait()
    whole[y] = part[...] + across_in[...]

    copies = []
    for step in range(1, ycount):
        copies.append(
            exchange(
                whole.at[y], whole.at[y], s4.at[step - 1], r4.at[step - 1], at_y(along(step))
            )
        )
        copies[-1].start()
    forward(5, 7)
    for copy in copies:
        copy.wait()

    copy = exchange(whole, twin, s5, r5, sibling)
    copy.start()
    forward(7, chan_count // BLOCK)
    copy.wait()

    low = jnp.where(core == 0, whole[...], twin[...]).reshape(segs * SLOW // 2, FAST)
    high = jnp.where(core == 0, twin[...], whole[...]).reshape(segs * SLOW // 2, FAST)

    def store_source(at, real, imag):
        for seg in range(8):
            src, place = (at + seg) // seg_count, (at + seg) % seg_count
            source[0, place, src] = real[seg]
            source[1, place, src] = imag[seg]

    transform(jnp.concatenate([low, high], axis=0), None, first, second, twist, store_source)

    def one_channel(block, lead, target):
        real_rows, imag_rows = [], []
        for strip in range(SLOW // 16):
            rows = slice(strip * 16, strip * 16 + 16)
            real_sum = imag_sum = None
            for seg in range(seg_count):
                w_real = white[0, block, seg * BLOCK + lead, rows][None]
                w_imag = white[1, block, seg * BLOCK + lead, rows][None]
                s_real = source[0, seg, :, rows]
                s_imag = source[1, seg, :, rows]
                real_now = s_real * w_real + s_imag * w_imag
                imag_now = s_real * w_imag - s_imag * w_real
                real_sum = real_now if seg == 0 else real_sum + real_now
                imag_sum = imag_now if seg == 0 else imag_sum + imag_now
            real_rows.append(real_sum.astype(jnp.bfloat16))
            imag_rows.append(imag_sum.astype(jnp.bfloat16))
        both = jnp.concatenate(
            [jnp.concatenate(real_rows, axis=1), jnp.concatenate(imag_rows, axis=1)], axis=2
        ).reshape(NSRC * SLOW, 2 * FAST)
        v = jnp.dot(both, back[...], preferred_element_type=jnp.float32)
        v_real = v[:, :FAST].reshape(NSRC, SLOW, FAST)
        v_imag = v[:, FAST:].reshape(NSRC, SLOW, FAST)
        turn_cos = turn[0][None]
        turn_sin = turn[1][None]
        w_real = (v_real * turn_cos - v_imag * turn_sin).astype(jnp.bfloat16)
        w_imag = (v_real * turn_sin + v_imag * turn_cos).astype(jnp.bfloat16)
        tall = jnp.concatenate(
            [w_real.reshape(NSRC * SLOW, FAST), w_imag.reshape(NSRC * SLOW, FAST)], axis=0
        )
        lagged = jnp.dot(outer[...], tall, preferred_element_type=jnp.float32)
        target[...] = lagged.astype(jnp.bfloat16).reshape(NSRC, SLOW, FAST)

    per = parts.shape[2]

    def one_group(to):
        def one(index, carry):
            place = index // per
            which = index % per
            chan = per * (place * xcount + to) + which
            one_channel(chan // BLOCK, chan % BLOCK, parts.at[to, place, which])
            return carry

        lax.fori_loop(0, zcount * per, one, 0)

    copies = []
    for step in range(1, xcount):
        to = (sx + step) % xcount
        one_group(to)
        copies.append(
            exchange(parts.at[to], x_in.at[step - 1], s6.at[step - 1], r6.at[step - 1], at_xz(sz, to))
        )
        copies[-1].start()
    one_group(sx)
    for copy in copies:
        copy.wait()

    def add_up(place):
        total = parts[sx, place].astype(jnp.float32)
        for step in range(xcount - 1):
            total = total + x_in[step, place].astype(jnp.float32)
        return total

    copies = []
    for step in range(1, zcount):
        to = (sz + step) % zcount
        mid[step - 1] = add_up(to).astype(jnp.bfloat16)
        copies.append(
            exchange(mid.at[step - 1], z_in.at[step - 1], s7.at[step - 1], r7.at[step - 1], at_xz(to, sx))
        )
        copies[-1].start()
    total = add_up(sz)
    for copy in copies:
        copy.wait()
    for step in range(zcount - 1):
        total = total + z_in[step].astype(jnp.float32)
    out[...] = total


def process(own, tiles, flags, ycount, xcount, zcount, out_scale):
    seg_count, chan_count = tiles.shape[:2]
    per = chan_count // (xcount * zcount)
    rows = NSRC * seg_count * SLOW
    slab = rows // (2 * ycount)
    dtype = own.dtype
    shaped = own.reshape(2, ycount, slab, FAST)
    half = (ycount, slab, FAST)
    result = (per, NSRC, SLOW, FAST)
    dma = pltpu.SemaphoreType.DMA
    vmem = pltpu.VMEM
    spec = pl.BlockSpec(memory_space=pltpu.VMEM)
    operands = (shaped, tiles, flags, jnp.eye(chan_count, dtype=jnp.float32)) + tables(out_scale)
    return pl.pallas_call(
        functools.partial(whole_kernel, ycount, xcount, zcount),
        out_shape=jax.ShapeDtypeStruct(result, jnp.float32),
        in_specs=[spec] * len(operands),
        out_specs=spec,
        scratch_shapes=[
            vmem((2, chan_count // BLOCK, BLOCK * seg_count, SLOW, FAST), jnp.float32),
            vmem((2, seg_count, NSRC, SLOW, FAST), jnp.float32),
            vmem((chan_count // BLOCK, BLOCK * seg_count, FAST), jnp.float32),
            vmem(half, dtype),
            vmem(half, dtype),
            vmem((ycount - 1, slab, FAST), dtype),
            vmem((slab, FAST), dtype),
            vmem((slab, FAST), dtype),
            vmem(half, dtype),
            vmem(half, dtype),
            vmem((xcount, zcount) + result, dtype),
            vmem((xcount - 1, zcount) + result, dtype),
            vmem((zcount - 1,) + result, dtype),
            vmem((zcount - 1,) + result, dtype),
            dma,
            dma,
            dma((ycount - 1,)),
            dma((ycount - 1,)),
            dma,
            dma,
            dma((ycount - 1,)),
            dma((ycount - 1,)),
            dma,
            dma,
            dma((xcount - 1,)),
            dma((xcount - 1,)),
            dma((zcount - 1,)),
            dma((zcount - 1,)),
        ],
        compiler_params=pltpu.CompilerParams(
            collective_id=0, has_side_effects=True, vmem_limit_bytes=VMEM_LIMIT
        ),
        name="process",
    )(*operands)


def pick_kernel(src, flags, tiles, out):
    seg_count, chan_count = tiles.shape[0], flags.shape[1]
    want = src[pl.program_id(0)]
    here = want // chan_count == lax.axis_index("chan")
    row = want % chan_count
    for seg in range(seg_count):
        keep = here & (flags[seg, row] != 0)
        factor = jnp.where(keep, 1.0, 0.0)
        out[0, seg] = (tiles[seg, 0].astype(jnp.float32) * factor).astype(out.dtype)


def pick(tiled, flags, src_chan):
    seg_count, chan_count = tiled.shape[:2]
    return pl.pallas_call(
        pick_kernel,
        grid_spec=pltpu.PrefetchScalarGridSpec(
            num_scalar_prefetch=2,
            grid=(NSRC,),
            in_specs=[
                pl.BlockSpec(
                    (seg_count, 1, SLOW, FAST),
                    lambda i, src, flags: (0, src[i] % chan_count, 0, 0),
                )
            ],
            out_specs=pl.BlockSpec(
                (1, seg_count, SLOW, FAST), lambda i, src, flags: (i, 0, 0, 0)
            ),
        ),
        out_shape=jax.ShapeDtypeStruct((NSRC, seg_count, SLOW, FAST), tiled.dtype),
        name="pick",
    )(src_chan, flags, tiled)


def per_device(recordings, valid_mask, src_chan):
    chan_count, seg_count, samples = recordings.shape
    group_count = lax.axis_size("tm")
    xcount = 4
    zcount = group_count // xcount
    ycount = lax.axis_size("chan") // 4
    out_scale = 1.0 / math.sqrt(samples * seg_count * group_count)
    tiled = jnp.transpose(recordings, (1, 0, 2)).reshape(seg_count, chan_count, SLOW, FAST)
    flags = jnp.transpose(valid_mask)
    mine = pick(tiled, flags, src_chan)
    summed = process(mine, tiled, flags, ycount, xcount, zcount, out_scale)
    return jnp.transpose(summed, (1, 0, 2, 3)).reshape(NSRC, chan_count // group_count, samples)


def solution(mesh):
    return jax.shard_map(
        per_device,
        mesh=mesh,
        in_specs=(P("chan", "tm", None), P("chan", "tm"), P()),
        out_specs=P(None, ("chan", "tm"), None),
        check_vma=False,
    )
```

```python
import functools
import math

import jax
import jax.numpy as jnp
import numpy as np
from jax import lax
from jax.experimental import pallas as pl
from jax.experimental.pallas import tpu as pltpu
from jax.sharding import PartitionSpec as P

NSRC = 4
SLOW = 32
FAST = 128
BLOCK = 6
MESH = pl.DeviceIdType.MESH
VMEM_LIMIT = 60 * 1024 * 1024


def angles(rows_count, cols_count, period):
    left_index = np.arange(rows_count)[:, None]
    right_index = np.arange(cols_count)[None, :]
    return 2.0 * math.pi / period * (left_index * right_index % period)


def tables(out_scale):
    slow = angles(SLOW, SLOW, SLOW)
    fast = angles(FAST, FAST, FAST)
    twist = angles(SLOW, FAST, SLOW * FAST)
    first = np.kron(np.eye(8), np.concatenate([np.cos(slow), -np.sin(slow)], axis=0))
    second = np.block([[np.cos(fast), -np.sin(fast)], [np.sin(fast), np.cos(fast)]])
    back = np.block([[np.cos(fast), np.sin(fast)], [-np.sin(fast), np.cos(fast)]])
    outer = np.concatenate(
        [np.kron(np.eye(NSRC), np.cos(slow)), np.kron(np.eye(NSRC), -np.sin(slow))], axis=1
    )
    return (
        jnp.asarray(first, jnp.bfloat16),
        jnp.asarray(
            first.reshape(-1, 8, SLOW).transpose(0, 2, 1).reshape(first.shape), jnp.bfloat16
        ),
        jnp.asarray(second, jnp.bfloat16),
        jnp.asarray(back, jnp.bfloat16),
        jnp.asarray(outer, jnp.bfloat16),
        jnp.asarray(np.stack([np.cos(twist), np.sin(twist)]), jnp.float32),
        jnp.asarray(np.stack([np.cos(twist), np.sin(twist)]) * out_scale, jnp.float32),
    )


def exchange(source, target, send, recv, device):
    return pltpu.make_async_remote_copy(
        src_ref=source,
        dst_ref=target,
        send_sem=send,
        recv_sem=recv,
        device_id=device,
        device_id_type=MESH,
    )


def greet(devices):
    barrier = pltpu.get_barrier_semaphore()
    for device in devices:
        pl.semaphore_signal(barrier, inc=1, device_id=device, device_id_type=MESH)
    return barrier, len(devices)


def transform(tiles, weight, first, second, twist, store):
    lane = lax.broadcasted_iota(jnp.int32, (8, FAST), 1)
    for pair in range(tiles.shape[0] // 2):
        wide = jnp.concatenate([tiles[2 * pair], tiles[2 * pair + 1]], axis=1)
        mixed = jnp.dot(first[...], wide, preferred_element_type=jnp.float32)
        for side in range(2):
            group = mixed[:, side * FAST : (side + 1) * FAST].reshape(8, 2 * SLOW, FAST)
            real_part = group[:, :SLOW]
            imag_part = group[:, SLOW:]
            twist_cos = twist[0][None]
            twist_sin = twist[1][None]
            z_real = (real_part * twist_cos + imag_part * twist_sin).astype(jnp.bfloat16)
            z_imag = (imag_part * twist_cos - real_part * twist_sin).astype(jnp.bfloat16)
            joined = jnp.concatenate([z_real, z_imag], axis=2).reshape(8 * SLOW, 2 * FAST)
            bins = jnp.dot(joined, second[...], preferred_element_type=jnp.float32)
            x_real = bins[:, :FAST].reshape(8, SLOW, FAST)
            x_imag = bins[:, FAST:].reshape(8, SLOW, FAST)
            power = jnp.sum(x_real * x_real + x_imag * x_imag, axis=1)
            other = jnp.where(
                lane % 2 == 0, pltpu.roll(power, FAST - 1, 1), pltpu.roll(power, 1, 1)
            )
            scale = lax.rsqrt((power + other) * (1.0 / (2 * SLOW)) + 1e-06)
            at = pair * 2 + side
            if weight is not None:
                scale = scale * weight(at)
            scale = scale[:, None, :]
            store(
                at,
                (x_real * scale).astype(jnp.bfloat16).astype(jnp.float32),
                (x_imag * scale).astype(jnp.bfloat16).astype(jnp.float32),
            )


def whole_kernel(
    ycount, xcount, zcount,
    src, marks, tiles, flags, eye, first, first_by_n, second, back, outer, twist, turn,
    out,
    white, source, weights, own,
    pair_in, half, slices_in, part, across_in, whole, twin,
    parts, x_in, mid, z_in,
    s1, r1, s2, r2, s3, r3, s4, r4, s5, r5, s6, r6, s7, r7,
):
    seg_count, chan_count = flags.shape
    sets = chan_count // 8
    me = lax.axis_index("chan")
    core = me % 2
    y = me // 2 % ycount
    z = me // (2 * ycount)
    sibling = {"chan": me - core + (1 - core)}
    opposite = {"chan": ((1 - z) * ycount + y) * 2 + core}
    spot = lax.axis_index("tm")
    sx = spot % xcount
    sz = spot // xcount

    def along(step):
        return (y + step) % ycount

    def at_y(place):
        return {"chan": (z * ycount + place) * 2 + core}

    def at_xz(zpos, xpos):
        return {"tm": zpos * xcount + xpos}

    barrier, count = greet(
        [sibling, opposite]
        + [at_y(along(step)) for step in range(1, ycount)]
        + [at_xz(sz, (sx + step) % xcount) for step in range(1, xcount)]
        + [at_xz((sz + step) % zcount, sx) for step in range(1, zcount)]
    )

    def forward(low, high):
        def one_block(block, carry):
            start = block * BLOCK

            def weight(at):
                return weights[start + at]

            def store(at, real, imag):
                seg = (start + at) // sets
                chan = (start + at) % sets * 8
                white[0, seg, pl.ds(chan, 8)] = real
                white[1, seg, pl.ds(chan, 8)] = imag

            transform(tiles[pl.ds(start, BLOCK)], weight, first_by_n, second, twist, store)
            return carry

        lax.fori_loop(low, high, one_block, 0)

    slot = lax.broadcasted_iota(jnp.int32, (SLOW, 8 * SLOW), 1)
    line = lax.broadcasted_iota(jnp.int32, (SLOW, 8 * SLOW), 0) * 8
    for index in range(NSRC):
        want = src[index]
        here = jnp.where(want // chan_count == me, 1, 0)
        row = want % chan_count
        chosen = jnp.where(slot == line + row % 8, 1.0, 0.0).astype(jnp.bfloat16)
        for seg in range(0, seg_count, 2):
            wide = jnp.concatenate(
                [tiles[seg * sets + row // 8], tiles[(seg + 1) * sets + row // 8]], axis=1
            )
            found = jnp.dot(chosen, wide, preferred_element_type=jnp.float32)
            for side in range(2):
                factor = (here * marks[seg + side, row]).astype(jnp.float32)
                place = (index % 2) * seg_count + seg + side
                per_slab = own.shape[2]
                own[index // 2, place // per_slab, place % per_slab] = (
                    found[:, side * FAST : (side + 1) * FAST] * factor
                ).astype(jnp.bfloat16)

    pl.semaphore_wait(barrier, count)
    copy = exchange(own.at[1 - core], pair_in, s1, r1, sibling)
    copy.start()
    spread = (flags[...].astype(jnp.float32)[:, None, :] * eye[...][None]).astype(jnp.bfloat16)
    rows = jnp.dot(
        spread.reshape(seg_count * chan_count, chan_count),
        jnp.ones((chan_count, FAST), jnp.bfloat16),
        preferred_element_type=jnp.float32,
    ).reshape(seg_count, chan_count, FAST)
    weights[...] = rows.reshape(seg_count * sets, 8, FAST)
    forward(0, 1)
    copy.wait()
    half[...] = own[core] + pair_in[...]

    copies = []
    for step in range(1, ycount):
        to = along(step)
        copies.append(
            exchange(half.at[to], slices_in.at[step - 1], s2.at[step - 1], r2.at[step - 1], at_y(to))
        )
        copies[-1].start()
    forward(1, 3)
    for copy in copies:
        copy.wait()
    total = half[y]
    for step in range(ycount - 1):
        total = total + slices_in[step]
    part[...] = total

    copy = exchange(part, across_in, s3, r3, opposite)
    copy.start()
    forward(3, 5)
    copy.wait()
    whole[y] = part[...] + across_in[...]

    copies = []
    for step in range(1, ycount):
        copies.append(
            exchange(
                whole.at[y], whole.at[y], s4.at[step - 1], r4.at[step - 1], at_y(along(step))
            )
        )
        copies[-1].start()
    forward(5, 7)
    for copy in copies:
        copy.wait()

    copy = exchange(whole, twin, s5, r5, sibling)
    copy.start()
    forward(7, seg_count * sets // BLOCK)
    copy.wait()

    low = jnp.where(core == 0, whole[...], twin[...])
    high = jnp.where(core == 0, twin[...], whole[...])

    def store_source(at, real, imag):
        for seg in range(8):
            index, place = (at * 8 + seg) // seg_count, (at * 8 + seg) % seg_count
            source[0, place, index] = real[seg]
            source[1, place, index] = real[seg] - imag[seg]
            source[2, place, index] = real[seg] + imag[seg]

    both_halves = jnp.concatenate([low, high], axis=0).reshape(-1, 8 * SLOW, FAST)
    transform(both_halves, None, first, second, twist, store_source)

    per = parts.shape[2]

    def some_channels(chan, to, place):
        real_rows = [[] for _ in range(per)]
        imag_rows = [[] for _ in range(per)]
        for strip in range(SLOW // 8):
            rows = slice(strip * 8, strip * 8 + 8)
            sums = [[None] * 3 for _ in range(per)]
            for seg in range(seg_count):
                terms = [source[k, seg, :, rows] for k in range(3)]
                for which in range(per):
                    w_real = white[0, seg, chan + which, rows]
                    w_imag = white[1, seg, chan + which, rows]
                    for k, factor in enumerate((w_real + w_imag, w_imag, w_real)):
                        now = terms[k] * factor[None]
                        sums[which][k] = now if seg == 0 else sums[which][k] + now
            for which in range(per):
                real_rows[which].append(sums[which][0] - sums[which][1])
                imag_rows[which].append(sums[which][0] - sums[which][2])
        both = jnp.concatenate(
            [
                jnp.concatenate(
                    [
                        jnp.concatenate(real_rows[which], axis=1).astype(jnp.bfloat16),
                        jnp.concatenate(imag_rows[which], axis=1).astype(jnp.bfloat16),
                    ],
                    axis=2,
                ).reshape(NSRC * SLOW, 2 * FAST)
                for which in range(per)
            ],
            axis=0,
        )
        v = jnp.dot(both, back[...], preferred_element_type=jnp.float32)
        v_real = v[:, :FAST].reshape(per * NSRC, SLOW, FAST)
        v_imag = v[:, FAST:].reshape(per * NSRC, SLOW, FAST)
        turn_cos = turn[0][None]
        turn_sin = turn[1][None]
        w_real = (v_real * turn_cos - v_imag * turn_sin).astype(jnp.bfloat16)
        w_imag = (v_real * turn_sin + v_imag * turn_cos).astype(jnp.bfloat16)
        w_real = w_real.reshape(per, NSRC * SLOW, FAST)
        w_imag = w_imag.reshape(per, NSRC * SLOW, FAST)
        tall = jnp.concatenate(
            [
                jnp.concatenate([w_real[which], w_imag[which]], axis=0)
                for which in range(per)
            ],
            axis=1,
        )
        lagged = jnp.dot(outer[...], tall, preferred_element_type=jnp.float32)
        for which in range(per):
            parts[to, place, which] = (
                lagged[:, which * FAST : (which + 1) * FAST]
                .astype(jnp.bfloat16)
                .reshape(NSRC, SLOW, FAST)
            )

    def one_group(to):
        def one(place, carry):
            some_channels(per * (place * xcount + to), to, place)
            return carry

        lax.fori_loop(0, zcount, one, 0)

    copies = []
    for step in range(1, xcount):
        to = (sx + step) % xcount
        one_group(to)
        copies.append(
            exchange(parts.at[to], x_in.at[step - 1], s6.at[step - 1], r6.at[step - 1], at_xz(sz, to))
        )
        copies[-1].start()
    one_group(sx)
    for copy in copies:
        copy.wait()

    def add_up(place):
        total = parts[sx, place].astype(jnp.float32)
        for step in range(xcount - 1):
            total = total + x_in[step, place].astype(jnp.float32)
        return total

    copies = []
    for step in range(1, zcount):
        to = (sz + step) % zcount
        mid[step - 1] = add_up(to).astype(jnp.bfloat16)
        copies.append(
            exchange(mid.at[step - 1], z_in.at[step - 1], s7.at[step - 1], r7.at[step - 1], at_xz(to, sx))
        )
        copies[-1].start()
    total = add_up(sz)
    for copy in copies:
        copy.wait()
    for step in range(zcount - 1):
        total = total + z_in[step].astype(jnp.float32)
    out[...] = total


def process(tiles, flags, src_chan, ycount, xcount, zcount, out_scale):
    seg_count, chan_count = flags.shape
    per = chan_count // (xcount * zcount)
    dtype = tiles.dtype
    slab = (NSRC * seg_count // (2 * ycount), SLOW, FAST)
    half = (ycount,) + slab
    result = (per, NSRC, SLOW, FAST)
    dma = pltpu.SemaphoreType.DMA
    vmem = pltpu.VMEM
    spec = pl.BlockSpec(memory_space=pltpu.VMEM)
    smem = pl.BlockSpec(memory_space=pltpu.SMEM)
    operands = (
        (tiles, flags, jnp.asarray(np.eye(chan_count), jnp.float32)) + tables(out_scale)
    )
    return pl.pallas_call(
        functools.partial(whole_kernel, ycount, xcount, zcount),
        out_shape=jax.ShapeDtypeStruct(result, jnp.float32),
        in_specs=[smem, smem] + [spec] * len(operands),
        out_specs=spec,
        scratch_shapes=[
            vmem((2, seg_count, chan_count, SLOW, FAST), jnp.float32),
            vmem((3, seg_count, NSRC, SLOW, FAST), jnp.float32),
            vmem((seg_count * chan_count // 8, 8, FAST), jnp.float32),
            vmem((2,) + half, dtype),
            vmem(half, dtype),
            vmem(half, dtype),
            vmem((ycount - 1,) + slab, dtype),
            vmem(slab, dtype),
            vmem(slab, dtype),
            vmem(half, dtype),
            vmem(half, dtype),
            vmem((xcount, zcount) + result, dtype),
            vmem((xcount - 1, zcount) + result, dtype),
            vmem((zcount - 1,) + result, dtype),
            vmem((zcount - 1,) + result, dtype),
            dma,
            dma,
            dma((ycount - 1,)),
            dma((ycount - 1,)),
            dma,
            dma,
            dma((ycount - 1,)),
            dma((ycount - 1,)),
            dma,
            dma,
            dma((xcount - 1,)),
            dma((xcount - 1,)),
            dma((zcount - 1,)),
            dma((zcount - 1,)),
        ],
        compiler_params=pltpu.CompilerParams(
            collective_id=0, has_side_effects=True, vmem_limit_bytes=VMEM_LIMIT
        ),
        name="process",
    )(src_chan, flags, *operands)


def per_device(recordings, valid_mask, src_chan):
    chan_count, seg_count, samples = recordings.shape
    group_count = lax.axis_size("tm")
    xcount = 4
    zcount = group_count // xcount
    ycount = lax.axis_size("chan") // 4
    out_scale = 1.0 / math.sqrt(samples * seg_count * group_count)
    tiles = jnp.transpose(recordings, (1, 0, 2))
    tiles = tiles.reshape(seg_count, chan_count // 8, 8, SLOW, FAST)
    tiles = jnp.transpose(tiles, (0, 1, 3, 2, 4))
    tiles = tiles.reshape(seg_count * chan_count // 8, 8 * SLOW, FAST)
    flags = jnp.transpose(valid_mask)
    summed = process(tiles, flags, src_chan, ycount, xcount, zcount, out_scale)
    return jnp.transpose(summed, (1, 0, 2, 3)).reshape(NSRC, chan_count // group_count, samples)


def solution(mesh):
    return jax.shard_map(
        per_device,
        mesh=mesh,
        in_specs=(P("chan", "tm", None), P("chan", "tm"), P()),
        out_specs=P(None, ("chan", "tm"), None),
        check_vma=False,
    )
```

```python
import functools
import math

import jax
import jax.numpy as jnp
import numpy as np
from jax import lax
from jax.experimental import pallas as pl
from jax.experimental.pallas import tpu as pltpu
from jax.sharding import PartitionSpec as P

NSRC = 4
SLOW = 32
FAST = 128
BLOCK = 6
UNROLL = 6
MESH = pl.DeviceIdType.MESH
VMEM_LIMIT = 60 * 1024 * 1024


def angles(rows_count, cols_count, period):
    left_index = np.arange(rows_count)[:, None]
    right_index = np.arange(cols_count)[None, :]
    return 2.0 * math.pi / period * (left_index * right_index % period)


def tables(out_scale):
    slow = angles(SLOW, SLOW, SLOW)
    fast = angles(FAST, FAST, FAST)
    twist = angles(SLOW, FAST, SLOW * FAST)
    first = np.kron(np.eye(8), np.concatenate([np.cos(slow), -np.sin(slow)], axis=0))
    second = np.block([[np.cos(fast), -np.sin(fast)], [np.sin(fast), np.cos(fast)]])
    back = np.block([[np.cos(fast), np.sin(fast)], [-np.sin(fast), np.cos(fast)]])
    outer = np.concatenate(
        [np.kron(np.eye(NSRC), np.cos(slow)), np.kron(np.eye(NSRC), -np.sin(slow))], axis=1
    )
    return (
        jnp.asarray(first, jnp.bfloat16),
        jnp.asarray(
            first.reshape(-1, 8, SLOW).transpose(0, 2, 1).reshape(first.shape), jnp.bfloat16
        ),
        jnp.asarray(second, jnp.bfloat16),
        jnp.asarray(back, jnp.bfloat16),
        jnp.asarray(outer, jnp.bfloat16),
        jnp.asarray(np.stack([np.cos(twist), np.sin(twist)]), jnp.float32),
        jnp.asarray(np.stack([np.cos(twist), np.sin(twist)]) * out_scale, jnp.float32),
    )


def exchange(source, target, send, recv, device):
    return pltpu.make_async_remote_copy(
        src_ref=source,
        dst_ref=target,
        send_sem=send,
        recv_sem=recv,
        device_id=device,
        device_id_type=MESH,
    )


def greet(devices):
    barrier = pltpu.get_barrier_semaphore()
    for device in devices:
        pl.semaphore_signal(barrier, inc=1, device_id=device, device_id_type=MESH)
    return barrier, len(devices)


def transform(tiles, weight, first, second, twist, store):
    lane = lax.broadcasted_iota(jnp.int32, (8, FAST), 1)
    for pair in range(tiles.shape[0] // 2):
        wide = jnp.concatenate([tiles[2 * pair], tiles[2 * pair + 1]], axis=1)
        mixed = jnp.dot(first[...], wide, preferred_element_type=jnp.float32)
        for side in range(2):
            group = mixed[:, side * FAST : (side + 1) * FAST].reshape(8, 2 * SLOW, FAST)
            real_part = group[:, :SLOW]
            imag_part = group[:, SLOW:]
            twist_cos = twist[0][None]
            twist_sin = twist[1][None]
            z_real = (real_part * twist_cos + imag_part * twist_sin).astype(jnp.bfloat16)
            z_imag = (imag_part * twist_cos - real_part * twist_sin).astype(jnp.bfloat16)
            joined = jnp.concatenate([z_real, z_imag], axis=2).reshape(8 * SLOW, 2 * FAST)
            bins = jnp.dot(joined, second[...], preferred_element_type=jnp.float32)
            x_real = bins[:, :FAST].reshape(8, SLOW, FAST)
            x_imag = bins[:, FAST:].reshape(8, SLOW, FAST)
            power = jnp.sum(x_real * x_real + x_imag * x_imag, axis=1)
            other = jnp.where(
                lane % 2 == 0, pltpu.roll(power, FAST - 1, 1), pltpu.roll(power, 1, 1)
            )
            scale = lax.rsqrt((power + other) * (1.0 / (2 * SLOW)) + 1e-06)
            at = pair * 2 + side
            if weight is not None:
                scale = scale * weight(at)
            scale = scale[:, None, :]
            store(
                at,
                (x_real * scale).astype(jnp.bfloat16).astype(jnp.float32),
                (x_imag * scale).astype(jnp.bfloat16).astype(jnp.float32),
            )


def whole_kernel(
    ycount, xcount, zcount,
    src, marks, tiles, flags, eye, first, first_by_n, second, back, outer, twist, turn,
    out,
    white, source, weights, own, cross,
    pair_in, half, slices_in, part, across_in, whole, twin,
    parts, x_in, mid, z_in,
    s1, r1, s2, r2, s3, r3, s4, r4, s5, r5, s6, r6, s7, r7,
):
    seg_count, chan_count = flags.shape
    sets = chan_count // 8
    me = lax.axis_index("chan")
    core = me % 2
    y = me // 2 % ycount
    z = me // (2 * ycount)
    sibling = {"chan": me - core + (1 - core)}
    opposite = {"chan": ((1 - z) * ycount + y) * 2 + core}
    spot = lax.axis_index("tm")
    sx = spot % xcount
    sz = spot // xcount

    def along(step):
        return (y + step) % ycount

    def at_y(place):
        return {"chan": (z * ycount + place) * 2 + core}

    def at_xz(zpos, xpos):
        return {"tm": zpos * xcount + xpos}

    barrier, count = greet(
        [sibling, opposite]
        + [at_y(along(step)) for step in range(1, ycount)]
        + [at_xz(sz, (sx + step) % xcount) for step in range(1, xcount)]
        + [at_xz((sz + step) % zcount, sx) for step in range(1, zcount)]
    )

    def forward(low, high):
        def one_block(block, carry):
            start = block * BLOCK

            def weight(at):
                return weights[start + at]

            def store(at, real, imag):
                seg = (start + at) // sets
                chan = (start + at) % sets * 8
                white[0, seg, pl.ds(chan, 8)] = real
                white[1, seg, pl.ds(chan, 8)] = imag

            transform(tiles[pl.ds(start, BLOCK)], weight, first_by_n, second, twist, store)
            return carry

        lax.fori_loop(low, high, one_block, 0)

    slot = lax.broadcasted_iota(jnp.int32, (SLOW, 8 * SLOW), 1)
    line = lax.broadcasted_iota(jnp.int32, (SLOW, 8 * SLOW), 0) * 8
    for index in range(NSRC):
        want = src[index]
        here = jnp.where(want // chan_count == me, 1, 0)
        row = want % chan_count
        chosen = jnp.where(slot == line + row % 8, 1.0, 0.0).astype(jnp.bfloat16)
        for seg in range(0, seg_count, 2):
            wide = jnp.concatenate(
                [tiles[seg * sets + row // 8], tiles[(seg + 1) * sets + row // 8]], axis=1
            )
            found = jnp.dot(chosen, wide, preferred_element_type=jnp.float32)
            for side in range(2):
                factor = (here * marks[seg + side, row]).astype(jnp.float32)
                place = (index % 2) * seg_count + seg + side
                per_slab = own.shape[2]
                own[index // 2, place // per_slab, place % per_slab] = (
                    found[:, side * FAST : (side + 1) * FAST] * factor
                ).astype(jnp.bfloat16)

    pl.semaphore_wait(barrier, count)
    copy = exchange(own.at[1 - core], pair_in, s1, r1, sibling)
    copy.start()
    spread = (flags[...].astype(jnp.float32)[:, None, :] * eye[...][None]).astype(jnp.bfloat16)
    rows = jnp.dot(
        spread.reshape(seg_count * chan_count, chan_count),
        jnp.ones((chan_count, FAST), jnp.bfloat16),
        preferred_element_type=jnp.float32,
    ).reshape(seg_count, chan_count, FAST)
    weights[...] = rows.reshape(seg_count * sets, 8, FAST)
    forward(0, 1)
    copy.wait()
    half[...] = own[core] + pair_in[...]

    copies = []
    for step in range(1, ycount):
        to = along(step)
        copies.append(
            exchange(half.at[to], slices_in.at[step - 1], s2.at[step - 1], r2.at[step - 1], at_y(to))
        )
        copies[-1].start()
    forward(1, 3)
    for copy in copies:
        copy.wait()
    total = half[y]
    for step in range(ycount - 1):
        total = total + slices_in[step]
    part[...] = total

    copy = exchange(part, across_in, s3, r3, opposite)
    copy.start()
    forward(3, 5)
    copy.wait()
    whole[y] = part[...] + across_in[...]

    copies = []
    for step in range(1, ycount):
        copies.append(
            exchange(
                whole.at[y], whole.at[y], s4.at[step - 1], r4.at[step - 1], at_y(along(step))
            )
        )
        copies[-1].start()
    forward(5, 7)
    for copy in copies:
        copy.wait()

    copy = exchange(whole, twin, s5, r5, sibling)
    copy.start()
    forward(7, seg_count * sets // BLOCK)
    copy.wait()

    low = jnp.where(core == 0, whole[...], twin[...])
    high = jnp.where(core == 0, twin[...], whole[...])

    def store_source(at, real, imag):
        for seg in range(8):
            index, place = (at * 8 + seg) // seg_count, (at * 8 + seg) % seg_count
            source[0, place, index] = real[seg]
            source[1, place, index] = real[seg] - imag[seg]
            source[2, place, index] = real[seg] + imag[seg]

    both_halves = jnp.concatenate([low, high], axis=0).reshape(-1, 8 * SLOW, FAST)
    transform(both_halves, None, first, second, twist, store_source)

    per = parts.shape[2]

    def some_channels(chan, place):
        def one_strip(strip, carry):
            rows = pl.ds(pl.multiple_of(strip * 8, 8), 8)

            def one_segment(seg, sums):
                terms = [source[k, seg, :, rows] for k in range(3)]
                new = []
                for which in range(per):
                    w_real = white[0, seg, chan + which, rows]
                    w_imag = white[1, seg, chan + which, rows]
                    for k, factor in enumerate((w_real + w_imag, w_imag, w_real)):
                        new.append(sums[3 * which + k] + terms[k] * factor[None])
                return tuple(new)

            zero = jnp.zeros((NSRC, 8, FAST), jnp.float32)
            sums = lax.fori_loop(0, seg_count, one_segment, (zero,) * (3 * per), unroll=UNROLL)
            for which in range(per):
                base, less, more = sums[3 * which : 3 * which + 3]
                cross[place, which, :, rows, :FAST] = base - less
                cross[place, which, :, rows, FAST:] = base - more
            return carry

        lax.fori_loop(0, SLOW // 8, one_strip, 0)

    def finish(to, place):
        both = cross[place].astype(jnp.bfloat16).reshape(per * NSRC * SLOW, 2 * FAST)
        v = jnp.dot(both, back[...], preferred_element_type=jnp.float32)
        v_real = v[:, :FAST].reshape(per * NSRC, SLOW, FAST)
        v_imag = v[:, FAST:].reshape(per * NSRC, SLOW, FAST)
        turn_cos = turn[0][None]
        turn_sin = turn[1][None]
        w_real = (v_real * turn_cos - v_imag * turn_sin).astype(jnp.bfloat16)
        w_imag = (v_real * turn_sin + v_imag * turn_cos).astype(jnp.bfloat16)
        w_real = w_real.reshape(per, NSRC * SLOW, FAST)
        w_imag = w_imag.reshape(per, NSRC * SLOW, FAST)
        tall = jnp.concatenate(
            [
                jnp.concatenate([w_real[which], w_imag[which]], axis=0)
                for which in range(per)
            ],
            axis=1,
        )
        lagged = jnp.dot(outer[...], tall, preferred_element_type=jnp.float32)
        for which in range(per):
            parts[to, place, which] = (
                lagged[:, which * FAST : (which + 1) * FAST]
                .astype(jnp.bfloat16)
                .reshape(NSRC, SLOW, FAST)
            )

    def one_group(to):
        def one(place, carry):
            some_channels(per * (place * xcount + to), place)
            return carry

        lax.fori_loop(0, zcount, one, 0)
        for place in range(zcount):
            finish(to, place)

    copies = []
    for step in range(1, xcount):
        to = (sx + step) % xcount
        one_group(to)
        copies.append(
            exchange(parts.at[to], x_in.at[step - 1], s6.at[step - 1], r6.at[step - 1], at_xz(sz, to))
        )
        copies[-1].start()
    one_group(sx)
    for copy in copies:
        copy.wait()

    def add_up(place):
        total = parts[sx, place].astype(jnp.float32)
        for step in range(xcount - 1):
            total = total + x_in[step, place].astype(jnp.float32)
        return total

    copies = []
    for step in range(1, zcount):
        to = (sz + step) % zcount
        mid[step - 1] = add_up(to).astype(jnp.bfloat16)
        copies.append(
            exchange(mid.at[step - 1], z_in.at[step - 1], s7.at[step - 1], r7.at[step - 1], at_xz(to, sx))
        )
        copies[-1].start()
    total = add_up(sz)
    for copy in copies:
        copy.wait()
    for step in range(zcount - 1):
        total = total + z_in[step].astype(jnp.float32)
    out[...] = total


def process(tiles, flags, src_chan, ycount, xcount, zcount, out_scale):
    seg_count, chan_count = flags.shape
    per = chan_count // (xcount * zcount)
    dtype = tiles.dtype
    slab = (NSRC * seg_count // (2 * ycount), SLOW, FAST)
    half = (ycount,) + slab
    result = (per, NSRC, SLOW, FAST)
    dma = pltpu.SemaphoreType.DMA
    vmem = pltpu.VMEM
    spec = pl.BlockSpec(memory_space=pltpu.VMEM)
    smem = pl.BlockSpec(memory_space=pltpu.SMEM)
    operands = (
        (tiles, flags, jnp.asarray(np.eye(chan_count), jnp.float32)) + tables(out_scale)
    )
    return pl.pallas_call(
        functools.partial(whole_kernel, ycount, xcount, zcount),
        out_shape=jax.ShapeDtypeStruct(result, jnp.float32),
        in_specs=[smem, smem] + [spec] * len(operands),
        out_specs=spec,
        scratch_shapes=[
            vmem((2, seg_count, chan_count, SLOW, FAST), jnp.float32),
            vmem((3, seg_count, NSRC, SLOW, FAST), jnp.float32),
            vmem((seg_count * chan_count // 8, 8, FAST), jnp.float32),
            vmem((2,) + half, dtype),
            vmem((zcount, per, NSRC, SLOW, 2 * FAST), jnp.float32),
            vmem(half, dtype),
            vmem(half, dtype),
            vmem((ycount - 1,) + slab, dtype),
            vmem(slab, dtype),
            vmem(slab, dtype),
            vmem(half, dtype),
            vmem(half, dtype),
            vmem((xcount, zcount) + result, dtype),
            vmem((xcount - 1, zcount) + result, dtype),
            vmem((zcount - 1,) + result, dtype),
            vmem((zcount - 1,) + result, dtype),
            dma,
            dma,
            dma((ycount - 1,)),
            dma((ycount - 1,)),
            dma,
            dma,
            dma((ycount - 1,)),
            dma((ycount - 1,)),
            dma,
            dma,
            dma((xcount - 1,)),
            dma((xcount - 1,)),
            dma((zcount - 1,)),
            dma((zcount - 1,)),
        ],
        compiler_params=pltpu.CompilerParams(
            collective_id=0, has_side_effects=True, vmem_limit_bytes=VMEM_LIMIT
        ),
        name="process",
    )(src_chan, flags, *operands)


def per_device(recordings, valid_mask, src_chan):
    chan_count, seg_count, samples = recordings.shape
    group_count = lax.axis_size("tm")
    xcount = 4
    zcount = group_count // xcount
    ycount = lax.axis_size("chan") // 4
    out_scale = 1.0 / math.sqrt(samples * seg_count * group_count)
    tiles = jnp.transpose(recordings, (1, 0, 2))
    tiles = tiles.reshape(seg_count, chan_count // 8, 8, SLOW, FAST)
    tiles = jnp.transpose(tiles, (0, 1, 3, 2, 4))
    tiles = tiles.reshape(seg_count * chan_count // 8, 8 * SLOW, FAST)
    flags = jnp.transpose(valid_mask)
    summed = process(tiles, flags, src_chan, ycount, xcount, zcount, out_scale)
    return jnp.transpose(summed, (1, 0, 2, 3)).reshape(NSRC, chan_count // group_count, samples)


def solution(mesh):
    return jax.shard_map(
        per_device,
        mesh=mesh,
        in_specs=(P("chan", "tm", None), P("chan", "tm"), P()),
        out_specs=P(None, ("chan", "tm"), None),
        check_vma=False,
    )
```

```python
import functools
import math

import jax
import jax.numpy as jnp
import numpy as np
from jax import lax
from jax.experimental import pallas as pl
from jax.experimental.pallas import tpu as pltpu
from jax.sharding import PartitionSpec as P

NSRC = 4
SLOW = 32
FAST = 128
BLOCK = 6
UNROLL = 6
MESH = pl.DeviceIdType.MESH
VMEM_LIMIT = 60 * 1024 * 1024


def angles(rows_count, cols_count, period):
    left_index = np.arange(rows_count)[:, None]
    right_index = np.arange(cols_count)[None, :]
    return 2.0 * math.pi / period * (left_index * right_index % period)


def tables(out_scale):
    slow = angles(SLOW, SLOW, SLOW)
    fast = angles(FAST, FAST, FAST)
    twist = angles(SLOW, FAST, SLOW * FAST)
    first = np.kron(np.eye(8), np.concatenate([np.cos(slow), -np.sin(slow)], axis=0))
    second = np.block([[np.cos(fast), -np.sin(fast)], [np.sin(fast), np.cos(fast)]])
    back = np.block([[np.cos(fast), np.sin(fast)], [-np.sin(fast), np.cos(fast)]])
    outer = np.concatenate(
        [np.kron(np.eye(NSRC), np.cos(slow)), np.kron(np.eye(NSRC), -np.sin(slow))], axis=1
    )
    return (
        jnp.asarray(first, jnp.bfloat16),
        jnp.asarray(
            first.reshape(-1, 8, SLOW).transpose(0, 2, 1).reshape(first.shape), jnp.bfloat16
        ),
        jnp.asarray(second, jnp.bfloat16),
        jnp.asarray(back, jnp.bfloat16),
        jnp.asarray(outer, jnp.bfloat16),
        jnp.asarray(np.stack([np.cos(twist), np.sin(twist)]), jnp.float32),
        jnp.asarray(np.stack([np.cos(twist), np.sin(twist)]) * out_scale, jnp.float32),
    )


def exchange(source, target, send, recv, device):
    return pltpu.make_async_remote_copy(
        src_ref=source,
        dst_ref=target,
        send_sem=send,
        recv_sem=recv,
        device_id=device,
        device_id_type=MESH,
    )


def greet(devices):
    barrier = pltpu.get_barrier_semaphore()
    for device in devices:
        pl.semaphore_signal(barrier, inc=1, device_id=device, device_id_type=MESH)
    return barrier, len(devices)


def transform(tiles, weight, first, second, twist, store):
    lane = lax.broadcasted_iota(jnp.int32, (8, FAST), 1)
    for pair in range(tiles.shape[0] // 2):
        wide = jnp.concatenate([tiles[2 * pair], tiles[2 * pair + 1]], axis=1)
        mixed = jnp.dot(first[...], wide, preferred_element_type=jnp.float32)
        for side in range(2):
            group = mixed[:, side * FAST : (side + 1) * FAST].reshape(8, 2 * SLOW, FAST)
            real_part = group[:, :SLOW]
            imag_part = group[:, SLOW:]
            twist_cos = twist[0][None]
            twist_sin = twist[1][None]
            z_real = (real_part * twist_cos + imag_part * twist_sin).astype(jnp.bfloat16)
            z_imag = (imag_part * twist_cos - real_part * twist_sin).astype(jnp.bfloat16)
            joined = jnp.concatenate([z_real, z_imag], axis=2).reshape(8 * SLOW, 2 * FAST)
            bins = jnp.dot(joined, second[...], preferred_element_type=jnp.float32)
            x_real = bins[:, :FAST].reshape(8, SLOW, FAST)
            x_imag = bins[:, FAST:].reshape(8, SLOW, FAST)
            power = jnp.sum(x_real * x_real + x_imag * x_imag, axis=1)
            other = jnp.where(
                lane % 2 == 0, pltpu.roll(power, FAST - 1, 1), pltpu.roll(power, 1, 1)
            )
            scale = lax.rsqrt((power + other) * (1.0 / (2 * SLOW)) + 1e-06)
            at = pair * 2 + side
            if weight is not None:
                scale = scale * weight(at)
            scale = scale[:, None, :]
            store(
                at,
                (x_real * scale).astype(jnp.bfloat16).astype(jnp.float32),
                (x_imag * scale).astype(jnp.bfloat16).astype(jnp.float32),
            )


def whole_kernel(
    ycount, xcount, zcount,
    src, marks, tiles, flags, eye, first, first_by_n, second, back, outer, twist, turn,
    out,
    white, source, weights, own, cross,
    pair_in, half, slices_in, part, across_in, whole, twin,
    parts, x_in, mid, z_in,
    s1, r1, s2, r2, s3, r3, s4, r4, s5, r5, s6, r6, s7, r7,
):
    seg_count, chan_count = flags.shape
    sets = chan_count // 8
    me = lax.axis_index("chan")
    core = me % 2
    y = me // 2 % ycount
    z = me // (2 * ycount)
    sibling = {"chan": me - core + (1 - core)}
    opposite = {"chan": ((1 - z) * ycount + y) * 2 + core}
    spot = lax.axis_index("tm")
    sx = spot % xcount
    sz = spot // xcount

    def along(step):
        return (y + step) % ycount

    def at_y(place):
        return {"chan": (z * ycount + place) * 2 + core}

    def at_xz(zpos, xpos):
        return {"tm": zpos * xcount + xpos}

    barrier, count = greet(
        [sibling, opposite]
        + [at_y(along(step)) for step in range(1, ycount)]
        + [at_xz(sz, (sx + step) % xcount) for step in range(1, xcount)]
        + [at_xz((sz + step) % zcount, sx) for step in range(1, zcount)]
    )

    def forward(low, high):
        def one_block(block, carry):
            start = block * BLOCK

            def weight(at):
                return weights[start + at]

            def store(at, real, imag):
                seg = (start + at) // sets
                chan = (start + at) % sets * 8
                white[0, seg, pl.ds(chan, 8)] = real
                white[1, seg, pl.ds(chan, 8)] = imag

            transform(tiles[pl.ds(start, BLOCK)], weight, first_by_n, second, twist, store)
            return carry

        lax.fori_loop(low, high, one_block, 0)

    slot = lax.broadcasted_iota(jnp.int32, (SLOW, 8 * SLOW), 1)
    line = lax.broadcasted_iota(jnp.int32, (SLOW, 8 * SLOW), 0) * 8
    for index in range(NSRC):
        want = src[index]
        here = jnp.where(want // chan_count == me, 1, 0)
        row = want % chan_count
        chosen = jnp.where(slot == line + row % 8, 1.0, 0.0).astype(jnp.bfloat16)
        for seg in range(0, seg_count, 2):
            wide = jnp.concatenate(
                [tiles[seg * sets + row // 8], tiles[(seg + 1) * sets + row // 8]], axis=1
            )
            found = jnp.dot(chosen, wide, preferred_element_type=jnp.float32)
            for side in range(2):
                factor = (here * marks[seg + side, row]).astype(jnp.float32)
                place = (index % 2) * seg_count + seg + side
                per_slab = own.shape[2]
                own[index // 2, place // per_slab, place % per_slab] = (
                    found[:, side * FAST : (side + 1) * FAST] * factor
                ).astype(jnp.bfloat16)

    pl.semaphore_wait(barrier, count)
    copy = exchange(own.at[1 - core], pair_in, s1, r1, sibling)
    copy.start()
    spread = (flags[...].astype(jnp.float32)[:, None, :] * eye[...][None]).astype(jnp.bfloat16)
    rows = jnp.dot(
        spread.reshape(seg_count * chan_count, chan_count),
        jnp.ones((chan_count, FAST), jnp.bfloat16),
        preferred_element_type=jnp.float32,
    ).reshape(seg_count, chan_count, FAST)
    weights[...] = rows.reshape(seg_count * sets, 8, FAST)
    forward(0, 1)
    copy.wait()
    half[...] = own[core] + pair_in[...]

    copies = []
    for step in range(1, ycount):
        to = along(step)
        copies.append(
            exchange(half.at[to], slices_in.at[step - 1], s2.at[step - 1], r2.at[step - 1], at_y(to))
        )
        copies[-1].start()
    forward(1, 3)
    for copy in copies:
        copy.wait()
    total = half[y]
    for step in range(ycount - 1):
        total = total + slices_in[step]
    part[...] = total

    copy = exchange(part, across_in, s3, r3, opposite)
    copy.start()
    forward(3, 5)
    copy.wait()
    whole[y] = part[...] + across_in[...]

    copies = []
    for step in range(1, ycount):
        copies.append(
            exchange(
                whole.at[y], whole.at[y], s4.at[step - 1], r4.at[step - 1], at_y(along(step))
            )
        )
        copies[-1].start()
    mirrors = [exchange(whole.at[y], twin.at[y], s5.at[0], r5.at[0], sibling)]
    mirrors[0].start()
    forward(5, 7)
    for step in range(1, ycount):
        copies[step - 1].wait_recv()
        came = (y + ycount - step) % ycount
        mirrors.append(
            exchange(whole.at[came], twin.at[came], s5.at[step], r5.at[step], sibling)
        )
        mirrors[-1].start()
    forward(7, seg_count * sets // BLOCK)
    for copy in copies:
        copy.wait_send()
    for copy in mirrors:
        copy.wait()

    low = jnp.where(core == 0, whole[...], twin[...])
    high = jnp.where(core == 0, twin[...], whole[...])

    def store_source(at, real, imag):
        for seg in range(8):
            index, place = (at * 8 + seg) // seg_count, (at * 8 + seg) % seg_count
            source[0, place, index] = real[seg]
            source[1, place, index] = real[seg] - imag[seg]
            source[2, place, index] = real[seg] + imag[seg]

    both_halves = jnp.concatenate([low, high], axis=0).reshape(-1, 8 * SLOW, FAST)
    transform(both_halves, None, first, second, twist, store_source)

    per = parts.shape[2]

    def some_channels(chan, place):
        def one_strip(strip, carry):
            rows = pl.ds(pl.multiple_of(strip * 8, 8), 8)

            def one_segment(seg, sums):
                terms = [source[k, seg, :, rows] for k in range(3)]
                new = []
                for which in range(per):
                    w_real = white[0, seg, chan + which, rows]
                    w_imag = white[1, seg, chan + which, rows]
                    for k, factor in enumerate((w_real + w_imag, w_imag, w_real)):
                        new.append(sums[3 * which + k] + terms[k] * factor[None])
                return tuple(new)

            zero = jnp.zeros((NSRC, 8, FAST), jnp.float32)
            sums = lax.fori_loop(0, seg_count, one_segment, (zero,) * (3 * per), unroll=UNROLL)
            for which in range(per):
                base, less, more = sums[3 * which : 3 * which + 3]
                cross[place, which, :, rows, :FAST] = base - less
                cross[place, which, :, rows, FAST:] = base - more
            return carry

        lax.fori_loop(0, SLOW // 8, one_strip, 0)

    def finish(to, place):
        both = cross[place].astype(jnp.bfloat16).reshape(per * NSRC * SLOW, 2 * FAST)
        v = jnp.dot(both, back[...], preferred_element_type=jnp.float32)
        v_real = v[:, :FAST].reshape(per * NSRC, SLOW, FAST)
        v_imag = v[:, FAST:].reshape(per * NSRC, SLOW, FAST)
        turn_cos = turn[0][None]
        turn_sin = turn[1][None]
        w_real = (v_real * turn_cos - v_imag * turn_sin).astype(jnp.bfloat16)
        w_imag = (v_real * turn_sin + v_imag * turn_cos).astype(jnp.bfloat16)
        w_real = w_real.reshape(per, NSRC * SLOW, FAST)
        w_imag = w_imag.reshape(per, NSRC * SLOW, FAST)
        tall = jnp.concatenate(
            [
                jnp.concatenate([w_real[which], w_imag[which]], axis=0)
                for which in range(per)
            ],
            axis=1,
        )
        lagged = jnp.dot(outer[...], tall, preferred_element_type=jnp.float32)
        for which in range(per):
            parts[to, place, which] = (
                lagged[:, which * FAST : (which + 1) * FAST]
                .astype(jnp.bfloat16)
                .reshape(NSRC, SLOW, FAST)
            )

    def one_group(to):
        def one(place, carry):
            some_channels(per * (place * xcount + to), place)
            return carry

        lax.fori_loop(0, zcount, one, 0)
        for place in range(zcount):
            finish(to, place)

    copies = []
    for step in range(1, xcount):
        to = (sx + step) % xcount
        one_group(to)
        copies.append(
            exchange(parts.at[to], x_in.at[step - 1], s6.at[step - 1], r6.at[step - 1], at_xz(sz, to))
        )
        copies[-1].start()
    one_group(sx)
    for copy in copies:
        copy.wait()

    def add_up(place):
        total = parts[sx, place].astype(jnp.float32)
        for step in range(xcount - 1):
            total = total + x_in[step, place].astype(jnp.float32)
        return total

    copies = []
    for step in range(1, zcount):
        to = (sz + step) % zcount
        mid[step - 1] = add_up(to).astype(jnp.bfloat16)
        copies.append(
            exchange(mid.at[step - 1], z_in.at[step - 1], s7.at[step - 1], r7.at[step - 1], at_xz(to, sx))
        )
        copies[-1].start()
    total = add_up(sz)
    for copy in copies:
        copy.wait()
    for step in range(zcount - 1):
        total = total + z_in[step].astype(jnp.float32)
    out[...] = total


def process(tiles, flags, src_chan, ycount, xcount, zcount, out_scale):
    seg_count, chan_count = flags.shape
    per = chan_count // (xcount * zcount)
    dtype = tiles.dtype
    slab = (NSRC * seg_count // (2 * ycount), SLOW, FAST)
    half = (ycount,) + slab
    result = (per, NSRC, SLOW, FAST)
    dma = pltpu.SemaphoreType.DMA
    vmem = pltpu.VMEM
    spec = pl.BlockSpec(memory_space=pltpu.VMEM)
    smem = pl.BlockSpec(memory_space=pltpu.SMEM)
    operands = (
        (tiles, flags, jnp.asarray(np.eye(chan_count), jnp.float32)) + tables(out_scale)
    )
    return pl.pallas_call(
        functools.partial(whole_kernel, ycount, xcount, zcount),
        out_shape=jax.ShapeDtypeStruct(result, jnp.float32),
        in_specs=[smem, smem] + [spec] * len(operands),
        out_specs=spec,
        scratch_shapes=[
            vmem((2, seg_count, chan_count, SLOW, FAST), jnp.float32),
            vmem((3, seg_count, NSRC, SLOW, FAST), jnp.float32),
            vmem((seg_count * chan_count // 8, 8, FAST), jnp.float32),
            vmem((2,) + half, dtype),
            vmem((zcount, per, NSRC, SLOW, 2 * FAST), jnp.float32),
            vmem(half, dtype),
            vmem(half, dtype),
            vmem((ycount - 1,) + slab, dtype),
            vmem(slab, dtype),
            vmem(slab, dtype),
            vmem(half, dtype),
            vmem(half, dtype),
            vmem((xcount, zcount) + result, dtype),
            vmem((xcount - 1, zcount) + result, dtype),
            vmem((zcount - 1,) + result, dtype),
            vmem((zcount - 1,) + result, dtype),
            dma,
            dma,
            dma((ycount - 1,)),
            dma((ycount - 1,)),
            dma,
            dma,
            dma((ycount - 1,)),
            dma((ycount - 1,)),
            dma((ycount,)),
            dma((ycount,)),
            dma((xcount - 1,)),
            dma((xcount - 1,)),
            dma((zcount - 1,)),
            dma((zcount - 1,)),
        ],
        compiler_params=pltpu.CompilerParams(
            collective_id=0, has_side_effects=True, vmem_limit_bytes=VMEM_LIMIT
        ),
        name="process",
    )(src_chan, flags, *operands)


def per_device(recordings, valid_mask, src_chan):
    chan_count, seg_count, samples = recordings.shape
    group_count = lax.axis_size("tm")
    xcount = 4
    zcount = group_count // xcount
    ycount = lax.axis_size("chan") // 4
    out_scale = 1.0 / math.sqrt(samples * seg_count * group_count)
    tiles = jnp.transpose(recordings, (1, 0, 2))
    tiles = tiles.reshape(seg_count, chan_count // 8, 8, SLOW, FAST)
    tiles = jnp.transpose(tiles, (0, 1, 3, 2, 4))
    tiles = tiles.reshape(seg_count * chan_count // 8, 8 * SLOW, FAST)
    flags = jnp.transpose(valid_mask)
    summed = process(tiles, flags, src_chan, ycount, xcount, zcount, out_scale)
    return jnp.transpose(summed, (1, 0, 2, 3)).reshape(NSRC, chan_count // group_count, samples)


def solution(mesh):
    return jax.shard_map(
        per_device,
        mesh=mesh,
        in_specs=(P("chan", "tm", None), P("chan", "tm"), P()),
        out_specs=P(None, ("chan", "tm"), None),
        check_vma=False,
    )
```
